32 devices in a mesh: space: 4 (over y, x), batch: 8 (over z, core).
Axes of the slice: x: 2, y: 2, z: 4, core: 2. Of those that a mesh axis runs over, the one named last changes fastest.
Arguments:
- pre_act: bfloat16 [8, 64, 4, 8, 128], P('batch', None, 'space'), may hold values from -6 to 6
- grad_out: bfloat16 [8, 128, 4, 8, 128], P('batch', None, 'space'), may hold values from -6 to 6
- weight: bfloat16 [27, 64, 128], replicated, may hold values from -0.109375 to 0.109375
Outputs:
- grad_in: bfloat16 [8, 64, 4, 8, 128], P('batch', None, 'space')
- weight_grad: float32 [221184], P(('space', 'batch'))
The draws below stay inside these ranges and needn't reach their ends.
All inputs are finite; a program needn't handle non-finite values.
Results may differ from the reference program's by a relative error of at most 0.001.
Values may be sent and summed in bfloat16 or wider, within the bound.
A program may use at most 64 MiB of HBM per device.

```python
import jax
import jax.numpy as jnp
from jax import lax

CIN = 64
COUT = 128
YC = 8
ZC = 128
SAMPLES = 8
NX = 4


def block_scale(stream_key, dims, pieces, least, high):
    loudness, own = 1.0, jax.random.fold_in(stream_key, 6)
    for dim, shards_of in pieces:
        draws = jnp.exp(jax.random.uniform(jax.random.fold_in(own, dim), (shards_of,), jnp.float32, least / len(pieces), high / len(pieces)))
        loudness = loudness * jnp.repeat(draws, dims[dim] // shards_of).reshape([-1 if axis == dim else 1 for axis in range(len(dims))])
    return loudness


def normal_values(key, extent, scale, most, pieces=(), dtype=jnp.bfloat16):
    values = jax.random.normal(key, extent, jnp.float32) * scale
    if len(pieces) > 0:
        values = block_scale(key, extent, pieces, -0.22, 0.18) * values
    return jnp.clip(values, min=-most, max=most).astype(dtype)


def setup_inputs(seed: int = 0) -> dict:
    key_list = jax.random.split(jax.random.key(seed), 4)
    return {
        "pre_act": normal_values(key_list[0], (SAMPLES, CIN, NX, YC, ZC), 1.0, 6.0, ((0, 8), (2, 4))),
        "grad_out": normal_values(key_list[1], (SAMPLES, COUT, NX, YC, ZC), 1.0, 6.0, ((0, 8), (2, 4))),
        "weight": normal_values(key_list[2], (27, CIN, COUT), (27 * COUT) ** -0.5, 0.109375),
    }


slope = 0.3

def reference(pre_act, grad_out, weight):
    factor = 1.0 / jnp.sqrt(jnp.float32(SAMPLES * NX * YC * ZC))
    kernel = weight.astype(jnp.float32)

    def per_sample(sample_pair):
        act_one, grad_one = sample_pair
        act_float = act_one.astype(jnp.float32)
        hidden = jnp.where(act_float > 0, act_float, slope * act_float).astype(jnp.bfloat16)
        hidden = lax.optimization_barrier(hidden).astype(jnp.float32)
        padded = jnp.pad(grad_one.astype(jnp.float32), ((0, 0), (1, 1), (1, 1), (1, 1)))
        grad_hidden = jnp.zeros((CIN, NX, YC, ZC), jnp.float32)
        tap_grads = []
        for tap in range(27):
            shift_x = tap // 9 - 1
            shift_y = tap // 3 % 3 - 1
            shift_z = tap % 3 - 1
            window = padded[:, 1 - shift_x:1 - shift_x + NX, 1 - shift_y:1 - shift_y + YC, 1 - shift_z:1 - shift_z + ZC]
            grad_hidden = grad_hidden + jnp.einsum('ic,cxyz->ixyz', kernel[tap], window, precision=lax.Precision.HIGHEST)
            tap_grads.append(jnp.einsum('ixyz,cxyz->ic', hidden, window, precision=lax.Precision.HIGHEST))
        grad_one_in = (grad_hidden * jnp.where(act_float > 0, 1.0, slope)).astype(jnp.bfloat16)
        return (grad_one_in, jnp.stack(tap_grads))
    grad_in, taps_all = lax.map(per_sample, (pre_act, grad_out))
    weight_grad = (lax.optimization_barrier(jnp.sum(taps_all, axis=0)) * factor).reshape(-1)
    return (grad_in, weight_grad)
```

```python
import functools

import jax
import jax.numpy as jnp
from jax import lax
from jax.experimental import pallas as pl
from jax.experimental.pallas import tpu as pltpu
from jax.sharding import PartitionSpec as P

slope = 0.3


def padded(block, sides, width):
    for axis, dim in sides:
        count = lax.axis_size(axis)
        forward = [(i, i + 1) for i in range(count - 1)]
        backward = [(target, source) for source, target in forward]
        low = lax.ppermute(
            lax.slice_in_dim(block, block.shape[dim] - width, None, axis=dim), axis, forward
        )
        high = lax.ppermute(lax.slice_in_dim(block, 0, width, axis=dim), axis, backward)
        block = jnp.concatenate([low, block, high], axis=dim)
    return block


def leaky(values):
    return jnp.where(values > 0, values, slope * values)


def on_device(pre_act, grad_out, weight):
    local_x = pre_act.shape[2]
    local_y = pre_act.shape[3]
    local_z = pre_act.shape[4]
    count = (
        pre_act.shape[0]
        * lax.axis_size("batch")
        * local_x
        * lax.axis_size("space")
        * local_y
        * local_z
    )
    factor = 1.0 / jnp.sqrt(jnp.float32(count))
    act_float = pre_act.astype(jnp.float32)
    yz_pad = ((0, 0), (0, 0), (0, 0), (1, 1), (1, 1))
    grad_hidden = jnp.zeros(pre_act.shape, jnp.float32)
    tap_grads = []
    joined = jnp.concatenate([pre_act, grad_out], axis=1)
    widened = padded(joined, (("space", 2),), 1)
    in_chan = pre_act.shape[1]
    hidden_pad = jnp.pad(
        leaky(widened[:, :in_chan].astype(jnp.float32)).astype(jnp.bfloat16), yz_pad
    )
    grad_pad = jnp.pad(widened[:, in_chan:], yz_pad)
    for tap in range(27):
        shift_x = tap // 9 - 1
        shift_y = tap // 3 % 3 - 1
        shift_z = tap % 3 - 1
        window = grad_pad[
            :,
            :,
            1 - shift_x : 1 - shift_x + local_x,
            1 - shift_y : 1 - shift_y + local_y,
            1 - shift_z : 1 - shift_z + local_z,
        ]
        grad_hidden = grad_hidden + jnp.einsum(
            "ic,scxyz->sixyz", weight[tap], window, preferred_element_type=jnp.float32
        )
        moved = hidden_pad[
            :,
            :,
            1 + shift_x : 1 + shift_x + local_x,
            1 + shift_y : 1 + shift_y + local_y,
            1 + shift_z : 1 + shift_z + local_z,
        ]
        tap_grads.append(
            jnp.einsum("sixyz,scxyz->ic", moved, grad_out, preferred_element_type=jnp.float32)
        )
    grad_in = (grad_hidden * jnp.where(act_float > 0, 1.0, slope)).astype(jnp.bfloat16)
    partial_sum = (jnp.stack(tap_grads) * factor).reshape(-1)
    space_part = lax.psum_scatter(partial_sum, "space", scatter_dimension=0, tiled=True)
    weight_grad = lax.psum_scatter(space_part, "batch", scatter_dimension=0, tiled=True)
    return (grad_in, weight_grad)


MESH = pl.DeviceIdType.MESH


def prepare(values, scratch, target):
    channels, rows, lanes = values.shape
    scratch[0 : channels * rows, :] = values.reshape(channels * rows, lanes)
    lane = lax.broadcasted_iota(jnp.int32, (channels, lanes), 1)
    blank = jnp.zeros((3 * channels, lanes), target.dtype)
    target[:, 0:lanes] = blank
    target[:, (rows + 1) * lanes : (rows + 2) * lanes] = blank
    for row in range(rows):
        block = scratch[pl.ds(row, channels, stride=rows), :]
        before = jnp.where(lane == 0, 0.0, pltpu.roll(block, 1, 1))
        after = jnp.where(lane == lanes - 1, 0.0, pltpu.roll(block, lanes - 1, 1))
        for place, shifted in enumerate((before, block, after)):
            target[
                place * channels : (place + 1) * channels, (row + 1) * lanes : (row + 2) * lanes
            ] = shifted.astype(target.dtype)


def halo_kernel(
    sizes,
    factor,
    pre_hbm,
    grad_hbm,
    weight_hbm,
    grad_in_ref,
    weight_grad_ref,
    pre_ref,
    grad_ref,
    weight_ref,
    pre_halo,
    grad_halo,
    plane,
    hidden_rows,
    grad_rows,
    total,
    partial,
    local_sem,
    direct_send,
    direct_recv,
    passed_send,
    passed_recv,
):
    space_count, batch_count = sizes
    space, batch = lax.axis_index("space"), lax.axis_index("batch")
    channels, rows, lanes = pre_ref.shape
    out_chan = grad_ref.shape[0]
    cells = rows * lanes

    coords = dict(c=lax.rem(batch, 2), z=batch // 2, x=lax.rem(space, 2), y=space // 2)
    side = coords["x"]

    def peer(axis, place):
        moved = dict(coords, **{axis: place})
        return (moved["y"] * 2 + moved["x"], moved["z"] * 2 + moved["c"])

    local = [
        pltpu.make_async_copy(source, target, local_sem.at[place])
        for place, (source, target) in enumerate(
            ((grad_hbm, grad_ref), (pre_hbm, pre_ref), (weight_hbm, weight_ref))
        )
    ]
    for copy in local:
        copy.start()

    barrier = pltpu.get_barrier_semaphore()
    low, high = space >= 2, space < space_count - 2
    pl.semaphore_signal(
        barrier, inc=1, device_id=peer("x", 1 - side), device_id_type=MESH
    )
    for there, condition in ((space - 2, low), (space + 2, high)):

        @pl.when(condition)
        def _():
            pl.semaphore_signal(barrier, inc=1, device_id=(there, batch), device_id_type=MESH)

    pl.semaphore_wait(barrier, 1 + jnp.where(low, 1, 0) + jnp.where(high, 1, 0))

    half, quarter = out_chan // 2, channels // 2
    messages = [
        (pre_hbm.at[0:quarter], lambda slot: pre_halo.at[slot, 0:quarter]),
        (pre_hbm.at[quarter:channels], lambda slot: pre_halo.at[slot, quarter:channels]),
        (grad_hbm.at[0:half], lambda slot: grad_halo.at[slot, 0:half]),
        (grad_hbm.at[half:out_chan], lambda slot: grad_halo.at[slot, half:out_chan]),
    ]
    near = 1 - side
    passes = jnp.where(side == 0, space < space_count - 2, space >= 2)
    gets = jnp.where(side == 0, space >= 2, space < space_count - 2)
    beyond = jnp.where(side == 0, space + 2, space - 2)

    def direct(index):
        source, slots = messages[index]
        return pltpu.make_async_remote_copy(
            src_ref=source,
            dst_ref=slots(side),
            send_sem=direct_send.at[index],
            recv_sem=direct_recv.at[index],
            device_id=peer("x", 1 - side),
            device_id_type=MESH,
        )

    def passed(index):
        slots = messages[index][1]
        return pltpu.make_async_remote_copy(
            src_ref=slots(near),
            dst_ref=slots(side),
            send_sem=passed_send.at[index],
            recv_sem=passed_recv.at[index],
            device_id=(beyond, batch),
            device_id_type=MESH,
        )

    sent = [direct(index) for index in range(4)]
    for copy in sent:
        copy.start()

    def pass_on(index):
        sent[index].wait_recv()

        @pl.when(passes)
        def _():
            passed(index).start()

    def take(first, target):
        @pl.when(gets)
        def _():
            passed(first).wait_recv()
            passed(first + 1).wait_recv()

        @pl.when(jnp.logical_not(gets))
        def _():
            target[side] = jnp.zeros(target.shape[1:], target.dtype)

    def hidden_plane(values, place):
        prepare(leaky(values.astype(jnp.float32)), plane, hidden_rows.at[place])

    def grad_plane(values, place):
        prepare(values.astype(jnp.float32), plane, grad_rows.at[place])

    def weight_terms(place):
        own = grad_rows[1, out_chan : 2 * out_chan, lanes : lanes + cells]
        for shift_y in (-1, 0, 1):
            start = (9 * place + 3 * (shift_y + 1)) * channels
            if not isinstance(place, int):
                start = pl.multiple_of(start, 8)
            term = lax.dot_general(
                hidden_rows[place, :, (1 + shift_y) * lanes : (1 + shift_y) * lanes + cells],
                own,
                (((1,), (1,)), ((), ())),
                preferred_element_type=jnp.float32,
            )
            partial[pl.ds(start, 3 * channels), :] = term * factor

    def input_terms(place, first):
        for shift_y in (-1, 0, 1):
            tap = 9 * (2 - place) + 3 * (shift_y + 1)
            term = jnp.dot(
                jnp.concatenate([weight_ref[tap + 2], weight_ref[tap + 1], weight_ref[tap]], axis=1),
                grad_rows[place, :, (1 - shift_y) * lanes : (1 - shift_y) * lanes + cells],
                preferred_element_type=jnp.float32,
            )
            if first and shift_y == -1:
                total[...] = term
            else:
                total[...] += term

    near_place, far_place = 2 * near, 2 * side

    local[0].wait()
    local[1].wait()
    grad_plane(grad_ref[...], 1)
    hidden_plane(pre_ref[...], 1)
    pass_on(0)
    pass_on(1)
    weight_terms(1)
    hidden_plane(pre_halo[near], near_place)
    weight_terms(near_place)
    local[2].wait()
    take(0, pre_halo)
    hidden_plane(pre_halo[side], far_place)
    weight_terms(far_place)

    def near_input():
        grad_plane(grad_halo[near], near_place)
        input_terms(near_place, False)

    def far_input():
        take(2, grad_halo)
        grad_plane(grad_halo[side], far_place)
        input_terms(far_place, False)
        for row in range(rows):
            plane[pl.ds(row, channels, stride=rows), :] = total[:, row * lanes : (row + 1) * lanes]
        back = plane[0 : channels * rows, :].reshape(channels, rows, lanes)
        act = pre_ref[...].astype(jnp.float32)
        grad_in_ref[...] = (back * jnp.where(act > 0, 1.0, slope)).astype(grad_in_ref.dtype)

    pass_on(2)
    pass_on(3)
    input_terms(1, True)
    near_input()
    far_input()
    weight_grad_ref[...] = partial[...]

    for copy in sent:
        copy.wait_send()

    @pl.when(passes)
    def _():
        for index in range(4):
            passed(index).wait_send()


class Plan:
    def __init__(self, space_count, batch_count, taps, channels):
        devices = space_count * batch_count
        self.section = taps * channels // 3
        self.piece = 3 * self.section // devices
        self.block = -(-self.piece // 8) * 8
        self.first, self.last, self.base, self.write, self.read = [], [], [], [], []
        for part in range(3):
            start = part * self.section
            first = start // self.piece
            self.first.append(first)
            self.last.append((start + self.section - 1) // self.piece)
            self.base.append(first - first % 2)
            ahead = start - self.piece * self.base[part]
            self.write.append(-(-ahead // 8) * 8)
            self.read.append(self.write[part] - ahead)
        self.count = max(
            (last - base) // 2 + 1 for last, base in zip(self.last, self.base, strict=True)
        )
        reach = self.piece * (2 * self.count - 1) + self.block
        self.rows = max(
            max(-(-(read + reach) // 8) * 8, write + self.section)
            for read, write in zip(self.read, self.write, strict=True)
        )


def plan_for(space_count, batch_count, taps, channels):
    devices = space_count * batch_count
    if space_count % 2 or batch_count % 2 or batch_count < 4 or space_count < 4:
        return None
    if taps % 3 or taps * channels % devices or taps * channels // devices < 8:
        return None
    plan = Plan(space_count, batch_count, taps, channels)
    if plan.read[0] or plan.read[2] or plan.last[0] >= plan.first[2]:
        return None
    return plan


def scatter_kernel(
    sizes,
    factor,
    plan,
    pre_hbm,
    grad_hbm,
    weight_hbm,
    grad_in_ref,
    weight_grad_ref,
    pre_ref,
    grad_ref,
    weight_ref,
    pre_halo,
    grad_halo,
    plane,
    hidden_rows,
    grad_rows,
    total,
    partial,
    held,
    arrived,
    summed,
    middle_in,
    outer_in,
    local_sem,
    pre_send,
    pre_recv,
    pre_pass_send,
    pre_pass_recv,
    grad_send,
    grad_recv,
    grad_pass_send,
    grad_pass_recv,
    core_send,
    core_recv,
    owner_send,
    middle_recv,
    outer_recv,
    ready,
):
    space_count, batch_count = sizes
    space, batch = lax.axis_index("space"), lax.axis_index("batch")
    channels, rows, lanes = pre_ref.shape
    out_chan = grad_ref.shape[0]
    cells = rows * lanes
    half_count, z_count = space_count // 2, batch_count // 2
    core, z = lax.rem(batch, 2), batch // 2
    side, line = lax.rem(space, 2), space // 2
    me = space * batch_count + batch
    near = 1 - side
    passes = jnp.where(side == 0, space < space_count - 2, space >= 2)
    gets = jnp.where(side == 0, space >= 2, space < space_count - 2)
    beyond = jnp.where(side == 0, space + 2, space - 2)
    across = (line * 2 + near, batch)
    twin = (space, z * 2 + 1 - core)

    group = [
        (lax.rem(line + step, half_count) * 2 + (side if straight else near), batch)
        for step in range(half_count)
        for straight in (True, False)
        if step or not straight
    ]
    barrier = pltpu.get_barrier_semaphore()
    column = [
        (space, lax.rem(z + step, z_count) * 2 + core) for step in range(1, z_count)
    ]
    for device in [twin, *group, *column]:
        pl.semaphore_signal(barrier, inc=1, device_id=device, device_id_type=MESH)

    local = [
        pltpu.make_async_copy(source, target, local_sem.at[place])
        for place, (source, target) in enumerate(
            ((grad_hbm, grad_ref), (pre_hbm, pre_ref), (weight_hbm, weight_ref))
        )
    ]
    for copy in local:
        copy.start()
    pl.semaphore_wait(barrier, 1 + len(group) + len(column))

    def crossing(source, halo, sems, passed_sems, width, index):
        cut = slice(index * width, (index + 1) * width)
        there = pltpu.make_async_remote_copy(
            src_ref=source.at[cut],
            dst_ref=halo.at[side, cut],
            send_sem=sems[0].at[index],
            recv_sem=sems[1].at[index],
            device_id=across,
            device_id_type=MESH,
        )
        onward = pltpu.make_async_remote_copy(
            src_ref=halo.at[near, cut],
            dst_ref=halo.at[side, cut],
            send_sem=passed_sems[0].at[index],
            recv_sem=passed_sems[1].at[index],
            device_id=(beyond, batch),
            device_id_type=MESH,
        )
        return there, onward

    pre_cuts, grad_cuts = pre_send.shape[0], grad_send.shape[0]
    pre_moves = [
        crossing(
            pre_hbm,
            pre_halo,
            (pre_send, pre_recv),
            (pre_pass_send, pre_pass_recv),
            channels // pre_cuts,
            index,
        )
        for index in range(pre_cuts)
    ]
    grad_moves = [
        crossing(
            grad_hbm,
            grad_halo,
            (grad_send, grad_recv),
            (grad_pass_send, grad_pass_recv),
            out_chan // grad_cuts,
            index,
        )
        for index in range(grad_cuts)
    ]

    def pass_on(move):
        move[0].wait_recv()

        @pl.when(passes)
        def _():
            move[1].start()

    for move in pre_moves:
        move[0].start()
    for device in group:
        pl.semaphore_signal(ready, inc=1, device_id=device, device_id_type=MESH)

    def weight_terms(place, phase, shift):
        own = grad_rows[1, out_chan : 2 * out_chan, lanes : lanes + cells]
        for shift_y in (-1, 0, 1):
            start = shift + 3 * (shift_y + 1) * channels
            if not isinstance(start, int):
                start = pl.multiple_of(start, 8)
            term = lax.dot_general(
                hidden_rows[place, :, (1 + shift_y) * lanes : (1 + shift_y) * lanes + cells],
                own,
                (((1,), (1,)), ((), ())),
                preferred_element_type=jnp.float32,
            )
            partial[phase, pl.ds(start, 3 * channels), :] = term * factor

    def input_terms(place, first):
        for shift_y in (-1, 0, 1):
            tap = 9 * (2 - place) + 3 * (shift_y + 1)
            term = jnp.dot(
                jnp.concatenate([weight_ref[tap + 2], weight_ref[tap + 1], weight_ref[tap]], axis=1),
                grad_rows[place, :, (1 - shift_y) * lanes : (1 - shift_y) * lanes + cells],
                preferred_element_type=jnp.float32,
            )
            if first and shift_y == -1:
                total[...] = term
            else:
                total[...] += term

    def hidden_plane(values, place):
        prepare(leaky(values.astype(jnp.float32)), plane, hidden_rows.at[place])

    def grad_plane(values, place):
        prepare(values.astype(jnp.float32), plane, grad_rows.at[place])

    def core_copy(phase):
        return pltpu.make_async_remote_copy(
            src_ref=held.at[phase, 1 - core],
            dst_ref=arrived.at[phase],
            send_sem=core_send.at[phase],
            recv_sem=core_recv.at[phase],
            device_id=twin,
            device_id_type=MESH,
        )

    def pack(phase, read):
        for parity in range(2):
            for step in range(plan.count):
                start = read + plan.piece * (2 * step + parity)
                held[phase, parity, step] = partial[phase, start : start + plan.block, :]

    def owner_copies(phase, middle, late):
        def pick(values):
            return values[1] if middle else jnp.where(late, values[2], values[0])

        base, first, last = pick(plan.base), pick(plan.first), pick(plan.last)
        if middle:
            slot, target, recv = space * z_count + z, middle_in, middle_recv
        else:
            slot, target, recv = (space - jnp.where(late, 0, 1)) * z_count + z, outer_in, outer_recv
        for step in range(plan.count):
            owner = base + 2 * step + core
            valid = jnp.logical_and(owner >= first, owner <= last)
            remote = pltpu.make_async_remote_copy(
                src_ref=summed.at[phase, step],
                dst_ref=target.at[slot],
                send_sem=owner_send.at[phase, step],
                recv_sem=recv,
                device_id=(owner // batch_count, lax.rem(owner, batch_count)),
                device_id_type=MESH,
            )
            own = pltpu.make_async_copy(summed.at[phase, step], target.at[slot], recv)
            yield (
                jnp.logical_and(valid, owner != me),
                remote,
                jnp.logical_and(valid, owner == me),
                own,
            )

    def spread(phase, copies):
        core_copy(phase).wait_recv()
        summed[phase] = held[phase, core] + arrived[phase]
        for away, remote, here, own in copies:
            pl.when(away)(remote.start)
            pl.when(here)(own.start)

    def drain(copies):
        for away, remote, _, _ in copies:
            pl.when(away)(remote.wait_send)

    near_place, far_place = 2 * near, 2 * side
    partial[...] = jnp.zeros(partial.shape, jnp.float32)

    local[0].wait()
    local[1].wait()
    grad_plane(grad_ref[...], 1)
    hidden_plane(pre_ref[...], 1)
    weight_terms(1, 0, plan.write[1])
    pack(0, plan.read[1])
    core_copy(0).start()
    for move in grad_moves:
        move[0].start()
    local[2].wait()
    input_terms(1, True)
    pl.semaphore_wait(ready, len(group))
    inner = list(owner_copies(0, True, None))
    spread(0, inner)

    for move in pre_moves:
        pass_on(move)
    hidden_plane(pre_halo[near], near_place)
    near_late = side == 0
    weight_terms(near_place, 1, jnp.where(near_late, plan.write[2], plan.write[0]))
    pack(1, 0)
    core_copy(1).start()
    pass_on(grad_moves[0])
    close = list(owner_copies(1, False, near_late))
    spread(1, close)
    pass_on(grad_moves[1])

    distant = list(owner_copies(2, False, jnp.logical_not(near_late)))

    @pl.when(gets)
    def _():
        for move in pre_moves:
            move[1].wait_recv()
        hidden_plane(pre_halo[side], far_place)
        weight_terms(far_place, 2, jnp.where(near_late, plan.write[0], plan.write[2]))
        pack(2, 0)
        core_copy(2).start()

    for move in grad_moves[2:-1]:
        pass_on(move)

    @pl.when(gets)
    def _():
        spread(2, distant)

    pass_on(grad_moves[-1])
    grad_plane(grad_halo[near], near_place)
    input_terms(near_place, False)

    @pl.when(gets)
    def _():
        for move in grad_moves:
            move[1].wait_recv()
        grad_plane(grad_halo[side], far_place)
        input_terms(far_place, False)

    for row in range(rows):
        plane[pl.ds(row, channels, stride=rows), :] = total[:, row * lanes : (row + 1) * lanes]
    back = plane[0 : channels * rows, :].reshape(channels, rows, lanes)
    act = pre_ref[...].astype(jnp.float32)
    grad_in_ref[...] = (back * jnp.where(act > 0, 1.0, slope)).astype(grad_in_ref.dtype)

    weight_grad_ref[...] = jnp.zeros(weight_grad_ref.shape, jnp.float32)

    def collect(condition, slots, recv):
        @pl.when(condition)
        def _():
            pltpu.make_async_copy(slots, slots, recv).wait()
            weight_grad_ref[...] += jnp.sum(slots[...], axis=0)

    collect(jnp.logical_and(me >= plan.first[1], me <= plan.last[1]), middle_in, middle_recv)
    collect(jnp.logical_or(me <= plan.last[0], me >= plan.first[2]), outer_in, outer_recv)

    for move in pre_moves + grad_moves:
        move[0].wait_send()
    core_copy(0).wait_send()
    core_copy(1).wait_send()
    drain(inner)
    drain(close)

    @pl.when(passes)
    def _():
        for move in pre_moves + grad_moves:
            move[1].wait_send()

    @pl.when(gets)
    def _():
        core_copy(2).wait_send()
        drain(distant)


def fused_device(pre_act, grad_out, weight):
    samples, channels, local_x, rows, lanes = pre_act.shape
    out_chan, taps = grad_out.shape[1], weight.shape[0]
    space_count, batch_count = lax.axis_size("space"), lax.axis_size("batch")
    fits = (
        samples == 1
        and local_x == 1
        and taps == 27
        and rows == 8
        and lanes == 128
        and out_chan == 128
        and channels % 64 == 0
        and space_count % 2 == 0
    )
    if not fits:
        return on_device(pre_act, grad_out, weight)
    count = samples * batch_count * local_x * space_count * rows * lanes
    factor = 1.0 / count**0.5
    total_rows = taps * channels
    plan = plan_for(space_count, batch_count, taps, channels)
    cells = rows * lanes
    widest = max(channels, out_chan)
    bf16, f32 = jnp.bfloat16, jnp.float32
    scratch = [
        pltpu.VMEM((channels, rows, lanes), bf16),
        pltpu.VMEM((out_chan, rows, lanes), bf16),
        pltpu.VMEM((taps, channels, out_chan), bf16),
        pltpu.VMEM((2, channels, rows, lanes), bf16),
        pltpu.VMEM((2, out_chan, rows, lanes), bf16),
        pltpu.VMEM((widest * rows, lanes), f32),
        pltpu.VMEM((3, 3 * channels, cells + 2 * lanes), bf16),
        pltpu.VMEM((3, 3 * out_chan, cells + 2 * lanes), bf16),
        pltpu.VMEM((channels, cells), f32),
    ]
    if plan:
        body = functools.partial(scatter_kernel, (space_count, batch_count), factor, plan)
        owned = plan.block
        block = (plan.block, out_chan)
        pre_cuts, grad_cuts = 4, 4
        scratch += [
            pltpu.VMEM((3, plan.rows, out_chan), f32),
            pltpu.VMEM((3, 2, plan.count, *block), f32),
            pltpu.VMEM((3, plan.count, *block), f32),
            pltpu.VMEM((3, plan.count, *block), f32),
            pltpu.VMEM((space_count * batch_count // 2, *block), f32),
            pltpu.VMEM(((space_count - 1) * batch_count // 2, *block), f32),
            pltpu.SemaphoreType.DMA((3,)),
            *[pltpu.SemaphoreType.DMA((pre_cuts,))] * 4,
            *[pltpu.SemaphoreType.DMA((grad_cuts,))] * 4,
            pltpu.SemaphoreType.DMA((3,)),
            pltpu.SemaphoreType.DMA((3,)),
            pltpu.SemaphoreType.DMA((3, plan.count)),
            pltpu.SemaphoreType.DMA,
            pltpu.SemaphoreType.DMA,
            pltpu.SemaphoreType.REGULAR,
        ]
    else:
        body = functools.partial(halo_kernel, (space_count, batch_count), factor)
        owned = total_rows
        scratch += [
            pltpu.VMEM((total_rows, out_chan), f32),
            *[pltpu.SemaphoreType.DMA((4,))] * 5,
        ]
    vmem = pl.BlockSpec(memory_space=pltpu.VMEM)
    grad_in, weight_grad = pl.pallas_call(
        body,
        out_shape=(
            jax.ShapeDtypeStruct((channels, rows, lanes), bf16),
            jax.ShapeDtypeStruct((owned, out_chan), f32),
        ),
        in_specs=[pl.BlockSpec(memory_space=pltpu.HBM)] * 3,
        out_specs=(vmem, vmem),
        scratch_shapes=scratch,
        compiler_params=pltpu.CompilerParams(
            collective_id=0, has_side_effects=True, vmem_limit_bytes=48 * 2**20
        ),
    )(
        pltpu.with_memory_space_constraint(pre_act.reshape(channels, rows, lanes), pltpu.HBM),
        pltpu.with_memory_space_constraint(grad_out.reshape(out_chan, rows, lanes), pltpu.HBM),
        pltpu.with_memory_space_constraint(weight, pltpu.HBM),
    )
    grad_in = grad_in.reshape(pre_act.shape)
    if plan:
        return grad_in, weight_grad[: plan.piece].reshape(-1)
    space_part = lax.psum_scatter(
        weight_grad.reshape(-1), "space", scatter_dimension=0, tiled=True
    )
    return grad_in, lax.psum_scatter(space_part, "batch", scatter_dimension=0, tiled=True)


def solution(mesh):
    return jax.shard_map(
        fused_device,
        mesh=mesh,
        in_specs=(
            P("batch", None, "space", None, None),
            P("batch", None, "space", None, None),
            P(),
        ),
        out_specs=(P("batch", None, "space", None, None), P(("space", "batch"))),
        check_vma=False,
    )
```

```python
import functools

import jax
import jax.numpy as jnp
from jax import lax
from jax.experimental import pallas as pl
from jax.experimental.pallas import tpu as pltpu
from jax.sharding import PartitionSpec as P

slope = 0.3


def padded(block, sides, width):
    for axis, dim in sides:
        count = lax.axis_size(axis)
        forward = [(i, i + 1) for i in range(count - 1)]
        backward = [(target, source) for source, target in forward]
        low = lax.ppermute(
            lax.slice_in_dim(block, block.shape[dim] - width, None, axis=dim), axis, forward
        )
        high = lax.ppermute(lax.slice_in_dim(block, 0, width, axis=dim), axis, backward)
        block = jnp.concatenate([low, block, high], axis=dim)
    return block


def leaky(values):
    return jnp.where(values > 0, values, slope * values)


def on_device(pre_act, grad_out, weight):
    local_x = pre_act.shape[2]
    local_y = pre_act.shape[3]
    local_z = pre_act.shape[4]
    count = (
        pre_act.shape[0]
        * lax.axis_size("batch")
        * local_x
        * lax.axis_size("space")
        * local_y
        * local_z
    )
    factor = 1.0 / jnp.sqrt(jnp.float32(count))
    act_float = pre_act.astype(jnp.float32)
    yz_pad = ((0, 0), (0, 0), (0, 0), (1, 1), (1, 1))
    grad_hidden = jnp.zeros(pre_act.shape, jnp.float32)
    tap_grads = []
    joined = jnp.concatenate([pre_act, grad_out], axis=1)
    widened = padded(joined, (("space", 2),), 1)
    in_chan = pre_act.shape[1]
    hidden_pad = jnp.pad(
        leaky(widened[:, :in_chan].astype(jnp.float32)).astype(jnp.bfloat16), yz_pad
    )
    grad_pad = jnp.pad(widened[:, in_chan:], yz_pad)
    for tap in range(27):
        shift_x = tap // 9 - 1
        shift_y = tap // 3 % 3 - 1
        shift_z = tap % 3 - 1
        window = grad_pad[
            :,
            :,
            1 - shift_x : 1 - shift_x + local_x,
            1 - shift_y : 1 - shift_y + local_y,
            1 - shift_z : 1 - shift_z + local_z,
        ]
        grad_hidden = grad_hidden + jnp.einsum(
            "ic,scxyz->sixyz", weight[tap], window, preferred_element_type=jnp.float32
        )
        moved = hidden_pad[
            :,
            :,
            1 + shift_x : 1 + shift_x + local_x,
            1 + shift_y : 1 + shift_y + local_y,
            1 + shift_z : 1 + shift_z + local_z,
        ]
        tap_grads.append(
            jnp.einsum("sixyz,scxyz->ic", moved, grad_out, preferred_element_type=jnp.float32)
        )
    grad_in = (grad_hidden * jnp.where(act_float > 0, 1.0, slope)).astype(jnp.bfloat16)
    partial_sum = (jnp.stack(tap_grads) * factor).reshape(-1)
    space_part = lax.psum_scatter(partial_sum, "space", scatter_dimension=0, tiled=True)
    weight_grad = lax.psum_scatter(space_part, "batch", scatter_dimension=0, tiled=True)
    return (grad_in, weight_grad)


MESH = pl.DeviceIdType.MESH


def prepare(values, scratch, target):
    channels, rows, lanes = values.shape
    scratch[0 : channels * rows, :] = values.reshape(channels * rows, lanes)
    lane = lax.broadcasted_iota(jnp.int32, (channels, lanes), 1)
    blank = jnp.zeros((3 * channels, lanes), target.dtype)
    target[:, 0:lanes] = blank
    target[:, (rows + 1) * lanes : (rows + 2) * lanes] = blank
    for row in range(rows):
        block = scratch[pl.ds(row, channels, stride=rows), :]
        before = jnp.where(lane == 0, 0.0, pltpu.roll(block, 1, 1))
        after = jnp.where(lane == lanes - 1, 0.0, pltpu.roll(block, lanes - 1, 1))
        for place, shifted in enumerate((before, block, after)):
            target[
                place * channels : (place + 1) * channels, (row + 1) * lanes : (row + 2) * lanes
            ] = shifted.astype(target.dtype)


def halo_kernel(
    sizes,
    factor,
    pre_hbm,
    grad_hbm,
    weight_hbm,
    grad_in_ref,
    weight_grad_ref,
    pre_ref,
    grad_ref,
    weight_ref,
    pre_halo,
    grad_halo,
    plane,
    hidden_rows,
    grad_rows,
    total,
    partial,
    local_sem,
    direct_send,
    direct_recv,
    passed_send,
    passed_recv,
):
    space_count, batch_count = sizes
    space, batch = lax.axis_index("space"), lax.axis_index("batch")
    channels, rows, lanes = pre_ref.shape
    out_chan = grad_ref.shape[0]
    cells = rows * lanes

    coords = dict(c=lax.rem(batch, 2), z=batch // 2, x=lax.rem(space, 2), y=space // 2)
    side = coords["x"]

    def peer(axis, place):
        moved = dict(coords, **{axis: place})
        return (moved["y"] * 2 + moved["x"], moved["z"] * 2 + moved["c"])

    local = [
        pltpu.make_async_copy(source, target, local_sem.at[place])
        for place, (source, target) in enumerate(
            ((grad_hbm, grad_ref), (pre_hbm, pre_ref), (weight_hbm, weight_ref))
        )
    ]
    for copy in local:
        copy.start()

    barrier = pltpu.get_barrier_semaphore()
    low, high = space >= 2, space < space_count - 2
    pl.semaphore_signal(
        barrier, inc=1, device_id=peer("x", 1 - side), device_id_type=MESH
    )
    for there, condition in ((space - 2, low), (space + 2, high)):

        @pl.when(condition)
        def _():
            pl.semaphore_signal(barrier, inc=1, device_id=(there, batch), device_id_type=MESH)

    pl.semaphore_wait(barrier, 1 + jnp.where(low, 1, 0) + jnp.where(high, 1, 0))

    half, quarter = out_chan // 2, channels // 2
    messages = [
        (pre_hbm.at[0:quarter], lambda slot: pre_halo.at[slot, 0:quarter]),
        (pre_hbm.at[quarter:channels], lambda slot: pre_halo.at[slot, quarter:channels]),
        (grad_hbm.at[0:half], lambda slot: grad_halo.at[slot, 0:half]),
        (grad_hbm.at[half:out_chan], lambda slot: grad_halo.at[slot, half:out_chan]),
    ]
    near = 1 - side
    passes = jnp.where(side == 0, space < space_count - 2, space >= 2)
    gets = jnp.where(side == 0, space >= 2, space < space_count - 2)
    beyond = jnp.where(side == 0, space + 2, space - 2)

    def direct(index):
        source, slots = messages[index]
        return pltpu.make_async_remote_copy(
            src_ref=source,
            dst_ref=slots(side),
            send_sem=direct_send.at[index],
            recv_sem=direct_recv.at[index],
            device_id=peer("x", 1 - side),
            device_id_type=MESH,
        )

    def passed(index):
        slots = messages[index][1]
        return pltpu.make_async_remote_copy(
            src_ref=slots(near),
            dst_ref=slots(side),
            send_sem=passed_send.at[index],
            recv_sem=passed_recv.at[index],
            device_id=(beyond, batch),
            device_id_type=MESH,
        )

    sent = [direct(index) for index in range(4)]
    for copy in sent:
        copy.start()

    def pass_on(index):
        sent[index].wait_recv()

        @pl.when(passes)
        def _():
            passed(index).start()

    def take(first, target):
        @pl.when(gets)
        def _():
            passed(first).wait_recv()
            passed(first + 1).wait_recv()

        @pl.when(jnp.logical_not(gets))
        def _():
            target[side] = jnp.zeros(target.shape[1:], target.dtype)

    def hidden_plane(values, place):
        prepare(leaky(values.astype(jnp.float32)), plane, hidden_rows.at[place])

    def grad_plane(values, place):
        prepare(values.astype(jnp.float32), plane, grad_rows.at[place])

    def weight_terms(place):
        own = grad_rows[1, out_chan : 2 * out_chan, lanes : lanes + cells]
        for shift_y in (-1, 0, 1):
            start = (9 * place + 3 * (shift_y + 1)) * channels
            if not isinstance(place, int):
                start = pl.multiple_of(start, 8)
            term = lax.dot_general(
                hidden_rows[place, :, (1 + shift_y) * lanes : (1 + shift_y) * lanes + cells],
                own,
                (((1,), (1,)), ((), ())),
                preferred_element_type=jnp.float32,
            )
            partial[pl.ds(start, 3 * channels), :] = term * factor

    def input_terms(place, first):
        for shift_y in (-1, 0, 1):
            tap = 9 * (2 - place) + 3 * (shift_y + 1)
            term = jnp.dot(
                jnp.concatenate([weight_ref[tap + 2], weight_ref[tap + 1], weight_ref[tap]], axis=1),
                grad_rows[place, :, (1 - shift_y) * lanes : (1 - shift_y) * lanes + cells],
                preferred_element_type=jnp.float32,
            )
            if first and shift_y == -1:
                total[...] = term
            else:
                total[...] += term

    near_place, far_place = 2 * near, 2 * side

    local[0].wait()
    local[1].wait()
    grad_plane(grad_ref[...], 1)
    hidden_plane(pre_ref[...], 1)
    pass_on(0)
    pass_on(1)
    weight_terms(1)
    hidden_plane(pre_halo[near], near_place)
    weight_terms(near_place)
    local[2].wait()
    take(0, pre_halo)
    hidden_plane(pre_halo[side], far_place)
    weight_terms(far_place)

    def near_input():
        grad_plane(grad_halo[near], near_place)
        input_terms(near_place, False)

    def far_input():
        take(2, grad_halo)
        grad_plane(grad_halo[side], far_place)
        input_terms(far_place, False)
        for row in range(rows):
            plane[pl.ds(row, channels, stride=rows), :] = total[:, row * lanes : (row + 1) * lanes]
        back = plane[0 : channels * rows, :].reshape(channels, rows, lanes)
        act = pre_ref[...].astype(jnp.float32)
        grad_in_ref[...] = (back * jnp.where(act > 0, 1.0, slope)).astype(grad_in_ref.dtype)

    pass_on(2)
    pass_on(3)
    input_terms(1, True)
    near_input()
    far_input()
    weight_grad_ref[...] = partial[...]

    for copy in sent:
        copy.wait_send()

    @pl.when(passes)
    def _():
        for index in range(4):
            passed(index).wait_send()


class Plan:
    def __init__(self, space_count, batch_count, taps, channels):
        devices = space_count * batch_count
        self.section = taps * channels // 3
        self.piece = 3 * self.section // devices
        self.block = -(-self.piece // 8) * 8
        self.first, self.last, self.base, self.write, self.read = [], [], [], [], []
        for part in range(3):
            start = part * self.section
            first = start // self.piece
            self.first.append(first)
            self.last.append((start + self.section - 1) // self.piece)
            self.base.append(first - first % 2)
            ahead = start - self.piece * self.base[part]
            self.write.append(-(-ahead // 8) * 8)
            self.read.append(self.write[part] - ahead)
        self.count = max(
            (last - base) // 2 + 1 for last, base in zip(self.last, self.base, strict=True)
        )
        reach = self.piece * (2 * self.count - 1) + self.block
        self.middle = {}
        for step in range(self.count):
            space, batch = divmod(self.base[1] + 2 * step, batch_count)
            self.middle.setdefault(space, []).append((step, batch // 2))
        self.rows = max(
            max(-(-(read + reach) // 8) * 8, write + self.section)
            for read, write in zip(self.read, self.write, strict=True)
        )


def plan_for(space_count, batch_count, taps, channels):
    devices = space_count * batch_count
    if space_count % 2 or batch_count % 2 or batch_count < 4 or space_count < 4:
        return None
    if taps % 3 or taps * channels % devices or taps * channels // devices < 8:
        return None
    plan = Plan(space_count, batch_count, taps, channels)
    if plan.read[0] or plan.read[2] or plan.last[0] >= plan.first[2]:
        return None
    if plan.first[1] != plan.base[1] or plan.last[1] != plan.base[1] + 2 * plan.count - 1:
        return None
    return plan


def scatter_kernel(
    sizes,
    factor,
    plan,
    pre_hbm,
    grad_hbm,
    weight_hbm,
    grad_in_ref,
    weight_grad_ref,
    pre_ref,
    grad_ref,
    weight_ref,
    pre_halo,
    grad_halo,
    plane,
    hidden_rows,
    grad_rows,
    total,
    partial,
    held,
    arrived,
    summed,
    column_in,
    column_sum,
    middle_in,
    outer_in,
    local_sem,
    pre_send,
    pre_recv,
    pre_pass_send,
    pre_pass_recv,
    grad_send,
    grad_recv,
    grad_pass_send,
    grad_pass_recv,
    core_send,
    core_recv,
    owner_send,
    plane_send,
    column_recv,
    middle_recv,
    outer_recv,
    ready,
):
    space_count, batch_count = sizes
    space, batch = lax.axis_index("space"), lax.axis_index("batch")
    channels, rows, lanes = pre_ref.shape
    out_chan = grad_ref.shape[0]
    cells = rows * lanes
    half_count, z_count = space_count // 2, batch_count // 2
    core, z = lax.rem(batch, 2), batch // 2
    side, line = lax.rem(space, 2), space // 2
    me = space * batch_count + batch
    near = 1 - side
    passes = jnp.where(side == 0, space < space_count - 2, space >= 2)
    gets = jnp.where(side == 0, space >= 2, space < space_count - 2)
    beyond = jnp.where(side == 0, space + 2, space - 2)
    across = (line * 2 + near, batch)
    twin = (space, z * 2 + 1 - core)

    group = [
        (lax.rem(line + step, half_count) * 2 + (side if straight else near), batch)
        for step in range(half_count)
        for straight in (True, False)
        if step or not straight
    ]
    barrier = pltpu.get_barrier_semaphore()
    column = [
        (space, lax.rem(z + step, z_count) * 2 + core) for step in range(1, z_count)
    ]
    for device in [twin, *group, *column]:
        pl.semaphore_signal(barrier, inc=1, device_id=device, device_id_type=MESH)

    local = [
        pltpu.make_async_copy(source, target, local_sem.at[place])
        for place, (source, target) in enumerate(
            ((grad_hbm, grad_ref), (pre_hbm, pre_ref), (weight_hbm, weight_ref))
        )
    ]
    for copy in local:
        copy.start()
    pl.semaphore_wait(barrier, 1 + len(group) + len(column))

    def crossing(source, halo, sems, passed_sems, width, index):
        cut = slice(index * width, (index + 1) * width)
        there = pltpu.make_async_remote_copy(
            src_ref=source.at[cut],
            dst_ref=halo.at[side, cut],
            send_sem=sems[0].at[index],
            recv_sem=sems[1].at[index],
            device_id=across,
            device_id_type=MESH,
        )
        onward = pltpu.make_async_remote_copy(
            src_ref=halo.at[near, cut],
            dst_ref=halo.at[side, cut],
            send_sem=passed_sems[0].at[index],
            recv_sem=passed_sems[1].at[index],
            device_id=(beyond, batch),
            device_id_type=MESH,
        )
        return there, onward

    pre_cuts, grad_cuts = pre_send.shape[0], grad_send.shape[0]
    pre_moves = [
        crossing(
            pre_hbm,
            pre_halo,
            (pre_send, pre_recv),
            (pre_pass_send, pre_pass_recv),
            channels // pre_cuts,
            index,
        )
        for index in range(pre_cuts)
    ]
    grad_moves = [
        crossing(
            grad_hbm,
            grad_halo,
            (grad_send, grad_recv),
            (grad_pass_send, grad_pass_recv),
            out_chan // grad_cuts,
            index,
        )
        for index in range(grad_cuts)
    ]

    def pass_on(move):
        move[0].wait_recv()

        @pl.when(passes)
        def _():
            move[1].start()

    for move in pre_moves:
        move[0].start()
    for device in group:
        pl.semaphore_signal(ready, inc=1, device_id=device, device_id_type=MESH)

    def weight_terms(place, phase, shift):
        own = grad_rows[1, out_chan : 2 * out_chan, lanes : lanes + cells]
        for shift_y in (-1, 0, 1):
            start = shift + 3 * (shift_y + 1) * channels
            if not isinstance(start, int):
                start = pl.multiple_of(start, 8)
            term = lax.dot_general(
                hidden_rows[place, :, (1 + shift_y) * lanes : (1 + shift_y) * lanes + cells],
                own,
                (((1,), (1,)), ((), ())),
                preferred_element_type=jnp.float32,
            )
            partial[phase, pl.ds(start, 3 * channels), :] = term * factor

    def input_terms(place, first):
        for shift_y in (-1, 0, 1):
            tap = 9 * (2 - place) + 3 * (shift_y + 1)
            term = jnp.dot(
                jnp.concatenate([weight_ref[tap + 2], weight_ref[tap + 1], weight_ref[tap]], axis=1),
                grad_rows[place, :, (1 - shift_y) * lanes : (1 - shift_y) * lanes + cells],
                preferred_element_type=jnp.float32,
            )
            if first and shift_y == -1:
                total[...] = term
            else:
                total[...] += term

    def hidden_plane(values, place):
        prepare(leaky(values.astype(jnp.float32)), plane, hidden_rows.at[place])

    def grad_plane(values, place):
        prepare(values.astype(jnp.float32), plane, grad_rows.at[place])

    def core_copy(phase):
        return pltpu.make_async_remote_copy(
            src_ref=held.at[phase, 1 - core],
            dst_ref=arrived.at[phase],
            send_sem=core_send.at[phase],
            recv_sem=core_recv.at[phase],
            device_id=twin,
            device_id_type=MESH,
        )

    def pack(phase, read):
        for parity in range(2):
            for step in range(plan.count):
                start = read + plan.piece * (2 * step + parity)
                held[phase, parity, step] = partial[phase, start : start + plan.block, :]

    def owner_copies(phase, late):
        def pick(values):
            return jnp.where(late, values[2], values[0])

        base, first, last = pick(plan.base), pick(plan.first), pick(plan.last)
        slot = (space - jnp.where(late, 0, 1)) * z_count + z
        for step in range(plan.count):
            owner = base + 2 * step + core
            valid = jnp.logical_and(owner >= first, owner <= last)
            remote = pltpu.make_async_remote_copy(
                src_ref=summed.at[phase, step],
                dst_ref=outer_in.at[slot],
                send_sem=owner_send.at[phase, step],
                recv_sem=outer_recv,
                device_id=(owner // batch_count, lax.rem(owner, batch_count)),
                device_id_type=MESH,
            )
            own = pltpu.make_async_copy(summed.at[phase, step], outer_in.at[slot], outer_recv)
            yield (
                jnp.logical_and(valid, owner != me),
                remote,
                jnp.logical_and(valid, owner == me),
                own,
            )

    def column_copies():
        for index, (there, steps) in enumerate(plan.middle.items()):
            for step, level in steps:
                yield z != level, pltpu.make_async_remote_copy(
                    src_ref=summed.at[0, step],
                    dst_ref=column_in.at[index, lax.rem(z - level + z_count, z_count) - 1],
                    send_sem=owner_send.at[0, step],
                    recv_sem=column_recv.at[index],
                    device_id=(space, level * 2 + core),
                    device_id_type=MESH,
                )

    def plane_copies():
        for index, (there, steps) in enumerate(plan.middle.items()):
            source, target = column_sum.at[index], middle_in.at[space]
            remote = pltpu.make_async_remote_copy(
                src_ref=source,
                dst_ref=target,
                send_sem=plane_send.at[index],
                recv_sem=middle_recv,
                device_id=(there, batch),
                device_id_type=MESH,
            )
            own = pltpu.make_async_copy(source, target, middle_recv)
            level, top = steps[0][1], steps[-1][1]
            here = jnp.logical_and(z >= level, z <= top)
            yield index, steps[0][0] + z - level, here, there, remote, own

    def send_middle():
        for index, step, here, there, remote, own in plane_copies():

            @pl.when(here)
            def _():
                got = column_in.at[index]
                pltpu.make_async_copy(got, got, column_recv.at[index]).wait()
                column_sum[index] = summed[0, step] + jnp.sum(got[...], axis=0)
                pl.when(space != there)(remote.start)
                pl.when(space == there)(own.start)

    def core_sum(phase):
        core_copy(phase).wait_recv()
        summed[phase] = held[phase, core] + arrived[phase]

    def spread(phase, copies):
        core_sum(phase)
        for away, remote, here, own in copies:
            pl.when(away)(remote.start)
            pl.when(here)(own.start)

    def drain(copies):
        for away, remote, _, _ in copies:
            pl.when(away)(remote.wait_send)

    near_place, far_place = 2 * near, 2 * side
    partial[...] = jnp.zeros(partial.shape, jnp.float32)

    local[0].wait()
    local[1].wait()
    grad_plane(grad_ref[...], 1)
    hidden_plane(pre_ref[...], 1)
    weight_terms(1, 0, plan.write[1])
    pack(0, plan.read[1])
    core_copy(0).start()
    local[2].wait()
    input_terms(1, True)
    core_sum(0)
    pl.semaphore_wait(ready, len(group))
    for away, copy in column_copies():
        pl.when(away)(copy.start)
    for move in grad_moves:
        move[0].start()

    for move in pre_moves:
        pass_on(move)
    hidden_plane(pre_halo[near], near_place)
    near_late = side == 0
    weight_terms(near_place, 1, jnp.where(near_late, plan.write[2], plan.write[0]))
    pack(1, 0)
    core_copy(1).start()
    close = list(owner_copies(1, near_late))
    spread(1, close)

    @pl.when(passes)
    def _():
        for move in grad_moves:
            move[0].wait_recv()
            move[1].start()

    distant = list(owner_copies(2, jnp.logical_not(near_late)))

    @pl.when(gets)
    def _():
        for move in pre_moves:
            move[1].wait_recv()
        hidden_plane(pre_halo[side], far_place)
        weight_terms(far_place, 2, jnp.where(near_late, plan.write[0], plan.write[2]))
        pack(2, 0)
        core_copy(2).start()

    send_middle()

    @pl.when(gets)
    def _():
        spread(2, distant)

    @pl.when(jnp.logical_not(passes))
    def _():
        for move in grad_moves:
            move[0].wait_recv()

    grad_plane(grad_halo[near], near_place)
    input_terms(near_place, False)

    @pl.when(gets)
    def _():
        for move in grad_moves:
            move[1].wait_recv()
        grad_plane(grad_halo[side], far_place)
        input_terms(far_place, False)

    for row in range(rows):
        plane[pl.ds(row, channels, stride=rows), :] = total[:, row * lanes : (row + 1) * lanes]
    back = plane[0 : channels * rows, :].reshape(channels, rows, lanes)
    act = pre_ref[...].astype(jnp.float32)
    grad_in_ref[...] = (back * jnp.where(act > 0, 1.0, slope)).astype(grad_in_ref.dtype)

    weight_grad_ref[...] = jnp.zeros(weight_grad_ref.shape, jnp.float32)

    def collect(condition, slots, recv):
        @pl.when(condition)
        def _():
            pltpu.make_async_copy(slots, slots, recv).wait()
            weight_grad_ref[...] += jnp.sum(slots[...], axis=0)

    collect(jnp.logical_and(me >= plan.first[1], me <= plan.last[1]), middle_in, middle_recv)
    collect(jnp.logical_or(me <= plan.last[0], me >= plan.first[2]), outer_in, outer_recv)

    for move in pre_moves + grad_moves:
        move[0].wait_send()
    core_copy(0).wait_send()
    core_copy(1).wait_send()
    for away, copy in column_copies():
        pl.when(away)(copy.wait_send)
    for _, _, here, there, remote, _ in plane_copies():
        pl.when(jnp.logical_and(here, space != there))(remote.wait_send)
    drain(close)

    @pl.when(passes)
    def _():
        for move in pre_moves + grad_moves:
            move[1].wait_send()

    @pl.when(gets)
    def _():
        core_copy(2).wait_send()
        drain(distant)


def fused_device(pre_act, grad_out, weight):
    samples, channels, local_x, rows, lanes = pre_act.shape
    out_chan, taps = grad_out.shape[1], weight.shape[0]
    space_count, batch_count = lax.axis_size("space"), lax.axis_size("batch")
    fits = (
        samples == 1
        and local_x == 1
        and taps == 27
        and rows == 8
        and lanes == 128
        and out_chan == 128
        and channels % 64 == 0
        and space_count % 2 == 0
    )
    if not fits:
        return on_device(pre_act, grad_out, weight)
    count = samples * batch_count * local_x * space_count * rows * lanes
    factor = 1.0 / count**0.5
    total_rows = taps * channels
    plan = plan_for(space_count, batch_count, taps, channels)
    cells = rows * lanes
    widest = max(channels, out_chan)
    bf16, f32 = jnp.bfloat16, jnp.float32
    scratch = [
        pltpu.VMEM((channels, rows, lanes), bf16),
        pltpu.VMEM((out_chan, rows, lanes), bf16),
        pltpu.VMEM((taps, channels, out_chan), bf16),
        pltpu.VMEM((2, channels, rows, lanes), bf16),
        pltpu.VMEM((2, out_chan, rows, lanes), bf16),
        pltpu.VMEM((widest * rows, lanes), f32),
        pltpu.VMEM((3, 3 * channels, cells + 2 * lanes), bf16),
        pltpu.VMEM((3, 3 * out_chan, cells + 2 * lanes), bf16),
        pltpu.VMEM((channels, cells), f32),
    ]
    if plan:
        body = functools.partial(scatter_kernel, (space_count, batch_count), factor, plan)
        owned = plan.block
        block = (plan.block, out_chan)
        pre_cuts, grad_cuts = 4, 4
        scratch += [
            pltpu.VMEM((3, plan.rows, out_chan), f32),
            pltpu.VMEM((3, 2, plan.count, *block), f32),
            pltpu.VMEM((3, plan.count, *block), f32),
            pltpu.VMEM((3, plan.count, *block), f32),
            pltpu.VMEM((len(plan.middle), batch_count // 2 - 1, *block), f32),
            pltpu.VMEM((len(plan.middle), *block), f32),
            pltpu.VMEM((space_count, *block), f32),
            pltpu.VMEM(((space_count - 1) * batch_count // 2, *block), f32),
            pltpu.SemaphoreType.DMA((3,)),
            *[pltpu.SemaphoreType.DMA((pre_cuts,))] * 4,
            *[pltpu.SemaphoreType.DMA((grad_cuts,))] * 4,
            pltpu.SemaphoreType.DMA((3,)),
            pltpu.SemaphoreType.DMA((3,)),
            pltpu.SemaphoreType.DMA((3, plan.count)),
            pltpu.SemaphoreType.DMA((len(plan.middle),)),
            pltpu.SemaphoreType.DMA((len(plan.middle),)),
            pltpu.SemaphoreType.DMA,
            pltpu.SemaphoreType.DMA,
            pltpu.SemaphoreType.REGULAR,
        ]
    else:
        body = functools.partial(halo_kernel, (space_count, batch_count), factor)
        owned = total_rows
        scratch += [
            pltpu.VMEM((total_rows, out_chan), f32),
            *[pltpu.SemaphoreType.DMA((4,))] * 5,
        ]
    vmem = pl.BlockSpec(memory_space=pltpu.VMEM)
    grad_in, weight_grad = pl.pallas_call(
        body,
        out_shape=(
            jax.ShapeDtypeStruct((channels, rows, lanes), bf16),
            jax.ShapeDtypeStruct((owned, out_chan), f32),
        ),
        in_specs=[pl.BlockSpec(memory_space=pltpu.HBM)] * 3,
        out_specs=(vmem, vmem),
        scratch_shapes=scratch,
        compiler_params=pltpu.CompilerParams(
            collective_id=0, has_side_effects=True, vmem_limit_bytes=48 * 2**20
        ),
    )(
        pltpu.with_memory_space_constraint(pre_act.reshape(channels, rows, lanes), pltpu.HBM),
        pltpu.with_memory_space_constraint(grad_out.reshape(out_chan, rows, lanes), pltpu.HBM),
        pltpu.with_memory_space_constraint(weight, pltpu.HBM),
    )
    grad_in = grad_in.reshape(pre_act.shape)
    if plan:
        return grad_in, weight_grad[: plan.piece].reshape(-1)
    space_part = lax.psum_scatter(
        weight_grad.reshape(-1), "space", scatter_dimension=0, tiled=True
    )
    return grad_in, lax.psum_scatter(space_part, "batch", scatter_dimension=0, tiled=True)


def solution(mesh):
    return jax.shard_map(
        fused_device,
        mesh=mesh,
        in_specs=(
            P("batch", None, "space", None, None),
            P("batch", None, "space", None, None),
            P(),
        ),
        out_specs=(P("batch", None, "space", None, None), P(("space", "batch"))),
        check_vma=False,
    )
```

```python
import functools

import jax
import jax.numpy as jnp
from jax import lax
from jax.experimental import pallas as pl
from jax.experimental.pallas import tpu as pltpu
from jax.sharding import PartitionSpec as P

slope = 0.3


def padded(block, sides, width):
    for axis, dim in sides:
        count = lax.axis_size(axis)
        forward = [(i, i + 1) for i in range(count - 1)]
        backward = [(target, source) for source, target in forward]
        low = lax.ppermute(
            lax.slice_in_dim(block, block.shape[dim] - width, None, axis=dim), axis, forward
        )
        high = lax.ppermute(lax.slice_in_dim(block, 0, width, axis=dim), axis, backward)
        block = jnp.concatenate([low, block, high], axis=dim)
    return block


def leaky(values):
    return jnp.where(values > 0, values, slope * values)


def on_device(pre_act, grad_out, weight):
    local_x = pre_act.shape[2]
    local_y = pre_act.shape[3]
    local_z = pre_act.shape[4]
    count = (
        pre_act.shape[0]
        * lax.axis_size("batch")
        * local_x
        * lax.axis_size("space")
        * local_y
        * local_z
    )
    factor = 1.0 / jnp.sqrt(jnp.float32(count))
    act_float = pre_act.astype(jnp.float32)
    yz_pad = ((0, 0), (0, 0), (0, 0), (1, 1), (1, 1))
    grad_hidden = jnp.zeros(pre_act.shape, jnp.float32)
    tap_grads = []
    joined = jnp.concatenate([pre_act, grad_out], axis=1)
    widened = padded(joined, (("space", 2),), 1)
    in_chan = pre_act.shape[1]
    hidden_pad = jnp.pad(
        leaky(widened[:, :in_chan].astype(jnp.float32)).astype(jnp.bfloat16), yz_pad
    )
    grad_pad = jnp.pad(widened[:, in_chan:], yz_pad)
    for tap in range(27):
        shift_x = tap // 9 - 1
        shift_y = tap // 3 % 3 - 1
        shift_z = tap % 3 - 1
        window = grad_pad[
            :,
            :,
            1 - shift_x : 1 - shift_x + local_x,
            1 - shift_y : 1 - shift_y + local_y,
            1 - shift_z : 1 - shift_z + local_z,
        ]
        grad_hidden = grad_hidden + jnp.einsum(
            "ic,scxyz->sixyz", weight[tap], window, preferred_element_type=jnp.float32
        )
        moved = hidden_pad[
            :,
            :,
            1 + shift_x : 1 + shift_x + local_x,
            1 + shift_y : 1 + shift_y + local_y,
            1 + shift_z : 1 + shift_z + local_z,
        ]
        tap_grads.append(
            jnp.einsum("sixyz,scxyz->ic", moved, grad_out, preferred_element_type=jnp.float32)
        )
    grad_in = (grad_hidden * jnp.where(act_float > 0, 1.0, slope)).astype(jnp.bfloat16)
    partial_sum = (jnp.stack(tap_grads) * factor).reshape(-1)
    space_part = lax.psum_scatter(partial_sum, "space", scatter_dimension=0, tiled=True)
    weight_grad = lax.psum_scatter(space_part, "batch", scatter_dimension=0, tiled=True)
    return (grad_in, weight_grad)


MESH = pl.DeviceIdType.MESH


def prepare(values, scratch, target):
    channels, rows, lanes = values.shape
    scratch[0 : channels * rows, :] = values.reshape(channels * rows, lanes)
    lane = lax.broadcasted_iota(jnp.int32, (channels, lanes), 1)
    blank = jnp.zeros((3 * channels, lanes), target.dtype)
    target[:, 0:lanes] = blank
    target[:, (rows + 1) * lanes : (rows + 2) * lanes] = blank
    for row in range(rows):
        block = scratch[pl.ds(row, channels, stride=rows), :]
        before = jnp.where(lane == 0, 0.0, pltpu.roll(block, 1, 1))
        after = jnp.where(lane == lanes - 1, 0.0, pltpu.roll(block, lanes - 1, 1))
        for place, shifted in enumerate((before, block, after)):
            target[
                place * channels : (place + 1) * channels, (row + 1) * lanes : (row + 2) * lanes
            ] = shifted.astype(target.dtype)


def halo_kernel(
    sizes,
    factor,
    pre_hbm,
    grad_hbm,
    weight_hbm,
    grad_in_ref,
    weight_grad_ref,
    pre_ref,
    grad_ref,
    weight_ref,
    pre_halo,
    grad_halo,
    plane,
    hidden_rows,
    grad_rows,
    total,
    partial,
    local_sem,
    direct_send,
    direct_recv,
    passed_send,
    passed_recv,
):
    space_count, batch_count = sizes
    space, batch = lax.axis_index("space"), lax.axis_index("batch")
    channels, rows, lanes = pre_ref.shape
    out_chan = grad_ref.shape[0]
    cells = rows * lanes

    coords = dict(c=lax.rem(batch, 2), z=batch // 2, x=lax.rem(space, 2), y=space // 2)
    side = coords["x"]

    def peer(axis, place):
        moved = dict(coords, **{axis: place})
        return (moved["y"] * 2 + moved["x"], moved["z"] * 2 + moved["c"])

    local = [
        pltpu.make_async_copy(source, target, local_sem.at[place])
        for place, (source, target) in enumerate(
            ((grad_hbm, grad_ref), (pre_hbm, pre_ref), (weight_hbm, weight_ref))
        )
    ]
    for copy in local:
        copy.start()

    barrier = pltpu.get_barrier_semaphore()
    low, high = space >= 2, space < space_count - 2
    pl.semaphore_signal(
        barrier, inc=1, device_id=peer("x", 1 - side), device_id_type=MESH
    )
    for there, condition in ((space - 2, low), (space + 2, high)):

        @pl.when(condition)
        def _():
            pl.semaphore_signal(barrier, inc=1, device_id=(there, batch), device_id_type=MESH)

    pl.semaphore_wait(barrier, 1 + jnp.where(low, 1, 0) + jnp.where(high, 1, 0))

    half, quarter = out_chan // 2, channels // 2
    messages = [
        (pre_hbm.at[0:quarter], lambda slot: pre_halo.at[slot, 0:quarter]),
        (pre_hbm.at[quarter:channels], lambda slot: pre_halo.at[slot, quarter:channels]),
        (grad_hbm.at[0:half], lambda slot: grad_halo.at[slot, 0:half]),
        (grad_hbm.at[half:out_chan], lambda slot: grad_halo.at[slot, half:out_chan]),
    ]
    near = 1 - side
    passes = jnp.where(side == 0, space < space_count - 2, space >= 2)
    gets = jnp.where(side == 0, space >= 2, space < space_count - 2)
    beyond = jnp.where(side == 0, space + 2, space - 2)

    def direct(index):
        source, slots = messages[index]
        return pltpu.make_async_remote_copy(
            src_ref=source,
            dst_ref=slots(side),
            send_sem=direct_send.at[index],
            recv_sem=direct_recv.at[index],
            device_id=peer("x", 1 - side),
            device_id_type=MESH,
        )

    def passed(index):
        slots = messages[index][1]
        return pltpu.make_async_remote_copy(
            src_ref=slots(near),
            dst_ref=slots(side),
            send_sem=passed_send.at[index],
            recv_sem=passed_recv.at[index],
            device_id=(beyond, batch),
            device_id_type=MESH,
        )

    sent = [direct(index) for index in range(4)]
    for copy in sent:
        copy.start()

    def pass_on(index):
        sent[index].wait_recv()

        @pl.when(passes)
        def _():
            passed(index).start()

    def take(first, target):
        @pl.when(gets)
        def _():
            passed(first).wait_recv()
            passed(first + 1).wait_recv()

        @pl.when(jnp.logical_not(gets))
        def _():
            target[side] = jnp.zeros(target.shape[1:], target.dtype)

    def hidden_plane(values, place):
        prepare(leaky(values.astype(jnp.float32)), plane, hidden_rows.at[place])

    def grad_plane(values, place):
        prepare(values.astype(jnp.float32), plane, grad_rows.at[place])

    def weight_terms(place):
        own = grad_rows[1, out_chan : 2 * out_chan, lanes : lanes + cells]
        for shift_y in (-1, 0, 1):
            start = (9 * place + 3 * (shift_y + 1)) * channels
            if not isinstance(place, int):
                start = pl.multiple_of(start, 8)
            term = lax.dot_general(
                hidden_rows[place, :, (1 + shift_y) * lanes : (1 + shift_y) * lanes + cells],
                own,
                (((1,), (1,)), ((), ())),
                preferred_element_type=jnp.float32,
            )
            partial[pl.ds(start, 3 * channels), :] = term * factor

    def input_terms(place, first):
        for shift_y in (-1, 0, 1):
            tap = 9 * (2 - place) + 3 * (shift_y + 1)
            term = jnp.dot(
                jnp.concatenate([weight_ref[tap + 2], weight_ref[tap + 1], weight_ref[tap]], axis=1),
                grad_rows[place, :, (1 - shift_y) * lanes : (1 - shift_y) * lanes + cells],
                preferred_element_type=jnp.float32,
            )
            if first and shift_y == -1:
                total[...] = term
            else:
                total[...] += term

    near_place, far_place = 2 * near, 2 * side

    local[0].wait()
    local[1].wait()
    grad_plane(grad_ref[...], 1)
    hidden_plane(pre_ref[...], 1)
    pass_on(0)
    pass_on(1)
    weight_terms(1)
    hidden_plane(pre_halo[near], near_place)
    weight_terms(near_place)
    local[2].wait()
    take(0, pre_halo)
    hidden_plane(pre_halo[side], far_place)
    weight_terms(far_place)

    def near_input():
        grad_plane(grad_halo[near], near_place)
        input_terms(near_place, False)

    def far_input():
        take(2, grad_halo)
        grad_plane(grad_halo[side], far_place)
        input_terms(far_place, False)
        for row in range(rows):
            plane[pl.ds(row, channels, stride=rows), :] = total[:, row * lanes : (row + 1) * lanes]
        back = plane[0 : channels * rows, :].reshape(channels, rows, lanes)
        act = pre_ref[...].astype(jnp.float32)
        grad_in_ref[...] = (back * jnp.where(act > 0, 1.0, slope)).astype(grad_in_ref.dtype)

    pass_on(2)
    pass_on(3)
    input_terms(1, True)
    near_input()
    far_input()
    weight_grad_ref[...] = partial[...]

    for copy in sent:
        copy.wait_send()

    @pl.when(passes)
    def _():
        for index in range(4):
            passed(index).wait_send()


class Plan:
    def __init__(self, space_count, batch_count, taps, channels):
        devices = space_count * batch_count
        self.section = taps * channels // 3
        self.piece = 3 * self.section // devices
        self.block = -(-self.piece // 8) * 8
        self.first, self.last, self.base, self.write, self.read = [], [], [], [], []
        for part in range(3):
            start = part * self.section
            first = start // self.piece
            self.first.append(first)
            self.last.append((start + self.section - 1) // self.piece)
            self.base.append(first - first % 2)
            ahead = start - self.piece * self.base[part]
            self.write.append(-(-ahead // 8) * 8)
            self.read.append(self.write[part] - ahead)
        self.count = max(
            (last - base) // 2 + 1 for last, base in zip(self.last, self.base, strict=True)
        )
        reach = self.piece * (2 * self.count - 1) + self.block
        self.turned = [
            [
                (step, owner // batch_count, owner % batch_count // 2)
                for step in range(self.count)
                for owner in [self.base[part] + 2 * step]
                if 0 < owner // batch_count < space_count - 1
                and owner + 1 >= self.first[part]
                and owner <= self.last[part]
            ]
            for part in range(3)
        ]
        self.middle = {}
        for step in range(self.count):
            space, batch = divmod(self.base[1] + 2 * step, batch_count)
            self.middle.setdefault(space, []).append((step, batch // 2))
        self.rows = max(
            max(-(-(read + reach) // 8) * 8, write + self.section)
            for read, write in zip(self.read, self.write, strict=True)
        )


def plan_for(space_count, batch_count, taps, channels):
    devices = space_count * batch_count
    if space_count % 2 or batch_count % 2 or batch_count < 4 or space_count < 4:
        return None
    if taps % 3 or taps * channels % devices or taps * channels // devices < 8:
        return None
    plan = Plan(space_count, batch_count, taps, channels)
    if plan.read[0] or plan.read[2] or plan.last[0] >= plan.first[2]:
        return None
    if len(plan.turned[0]) != len(plan.turned[2]) or not plan.turned[0]:
        return None
    for turned in (plan.turned[0], plan.turned[2]):
        if len({level for _, _, level in turned}) != len(turned):
            return None
    if plan.first[1] != plan.base[1] or plan.last[1] != plan.base[1] + 2 * plan.count - 1:
        return None
    return plan


def scatter_kernel(
    sizes,
    factor,
    plan,
    pre_hbm,
    grad_hbm,
    weight_hbm,
    grad_in_ref,
    weight_grad_ref,
    pre_ref,
    grad_ref,
    weight_ref,
    pre_halo,
    grad_halo,
    plane,
    hidden_rows,
    grad_rows,
    total,
    partial,
    held,
    arrived,
    summed,
    column_in,
    column_sum,
    middle_in,
    outer_in,
    turned_in,
    turned_sum,
    turned_out,
    local_sem,
    pre_send,
    pre_recv,
    pre_pass_send,
    pre_pass_recv,
    grad_send,
    grad_recv,
    grad_pass_send,
    grad_pass_recv,
    core_send,
    core_recv,
    owner_send,
    plane_send,
    column_recv,
    middle_recv,
    outer_recv,
    turned_send,
    turned_recv,
    turned_last,
    ready,
):
    space_count, batch_count = sizes
    space, batch = lax.axis_index("space"), lax.axis_index("batch")
    channels, rows, lanes = pre_ref.shape
    out_chan = grad_ref.shape[0]
    cells = rows * lanes
    half_count, z_count = space_count // 2, batch_count // 2
    core, z = lax.rem(batch, 2), batch // 2
    side, line = lax.rem(space, 2), space // 2
    me = space * batch_count + batch
    near = 1 - side
    passes = jnp.where(side == 0, space < space_count - 2, space >= 2)
    gets = jnp.where(side == 0, space >= 2, space < space_count - 2)
    beyond = jnp.where(side == 0, space + 2, space - 2)
    across = (line * 2 + near, batch)
    twin = (space, z * 2 + 1 - core)

    group = [
        (lax.rem(line + step, half_count) * 2 + (side if straight else near), batch)
        for step in range(half_count)
        for straight in (True, False)
        if step or not straight
    ]
    barrier = pltpu.get_barrier_semaphore()
    column = [
        (space, lax.rem(z + step, z_count) * 2 + core) for step in range(1, z_count)
    ]
    for device in [twin, *group, *column]:
        pl.semaphore_signal(barrier, inc=1, device_id=device, device_id_type=MESH)

    local = [
        pltpu.make_async_copy(source, target, local_sem.at[place])
        for place, (source, target) in enumerate(
            ((grad_hbm, grad_ref), (pre_hbm, pre_ref), (weight_hbm, weight_ref))
        )
    ]
    for copy in local:
        copy.start()
    pl.semaphore_wait(barrier, 1 + len(group) + len(column))

    def crossing(source, halo, sems, passed_sems, width, index):
        cut = slice(index * width, (index + 1) * width)
        there = pltpu.make_async_remote_copy(
            src_ref=source.at[cut],
            dst_ref=halo.at[side, cut],
            send_sem=sems[0].at[index],
            recv_sem=sems[1].at[index],
            device_id=across,
            device_id_type=MESH,
        )
        onward = pltpu.make_async_remote_copy(
            src_ref=halo.at[near, cut],
            dst_ref=halo.at[side, cut],
            send_sem=passed_sems[0].at[index],
            recv_sem=passed_sems[1].at[index],
            device_id=(beyond, batch),
            device_id_type=MESH,
        )
        return there, onward

    pre_cuts, grad_cuts = pre_send.shape[0], grad_send.shape[0]
    pre_moves = [
        crossing(
            pre_hbm,
            pre_halo,
            (pre_send, pre_recv),
            (pre_pass_send, pre_pass_recv),
            channels // pre_cuts,
            index,
        )
        for index in range(pre_cuts)
    ]
    grad_moves = [
        crossing(
            grad_hbm,
            grad_halo,
            (grad_send, grad_recv),
            (grad_pass_send, grad_pass_recv),
            out_chan // grad_cuts,
            index,
        )
        for index in range(grad_cuts)
    ]

    def pass_on(move):
        move[0].wait_recv()

        @pl.when(passes)
        def _():
            move[1].start()

    for move in pre_moves:
        move[0].start()
    for device in group:
        pl.semaphore_signal(ready, inc=1, device_id=device, device_id_type=MESH)

    def weight_terms(place, phase, shift):
        own = grad_rows[1, out_chan : 2 * out_chan, lanes : lanes + cells]
        for shift_y in (-1, 0, 1):
            start = shift + 3 * (shift_y + 1) * channels
            if not isinstance(start, int):
                start = pl.multiple_of(start, 8)
            term = lax.dot_general(
                hidden_rows[place, :, (1 + shift_y) * lanes : (1 + shift_y) * lanes + cells],
                own,
                (((1,), (1,)), ((), ())),
                preferred_element_type=jnp.float32,
            )
            partial[phase, pl.ds(start, 3 * channels), :] = term * factor

    def input_terms(place, first):
        for shift_y in (-1, 0, 1):
            tap = 9 * (2 - place) + 3 * (shift_y + 1)
            term = jnp.dot(
                jnp.concatenate([weight_ref[tap + 2], weight_ref[tap + 1], weight_ref[tap]], axis=1),
                grad_rows[place, :, (1 - shift_y) * lanes : (1 - shift_y) * lanes + cells],
                preferred_element_type=jnp.float32,
            )
            if first and shift_y == -1:
                total[...] = term
            else:
                total[...] += term

    def hidden_plane(values, place):
        prepare(leaky(values.astype(jnp.float32)), plane, hidden_rows.at[place])

    def grad_plane(values, place):
        prepare(values.astype(jnp.float32), plane, grad_rows.at[place])

    def core_copy(phase):
        return pltpu.make_async_remote_copy(
            src_ref=held.at[phase, 1 - core],
            dst_ref=arrived.at[phase],
            send_sem=core_send.at[phase],
            recv_sem=core_recv.at[phase],
            device_id=twin,
            device_id_type=MESH,
        )

    def pack(phase, read):
        for parity in range(2):
            for step in range(plan.count):
                start = read + plan.piece * (2 * step + parity)
                held[phase, parity, step] = partial[phase, start : start + plan.block, :]

    def owner_copies(phase, late):
        def pick(values):
            return jnp.where(late, values[2], values[0])

        base, first, last = pick(plan.base), pick(plan.first), pick(plan.last)
        far_slot = line - jnp.where(late, 0, 1)
        slot = (line if phase == 1 else half_count + far_slot) * z_count + z
        for step in range(plan.count):
            owner = base + 2 * step + core
            valid = jnp.logical_and(owner >= first, owner <= last)
            if phase == 2:
                valid = jnp.logical_and(
                    valid,
                    jnp.logical_or(
                        owner < batch_count, owner >= (space_count - 1) * batch_count
                    ),
                )
            remote = pltpu.make_async_remote_copy(
                src_ref=summed.at[phase, step],
                dst_ref=outer_in.at[slot],
                send_sem=owner_send.at[phase, step],
                recv_sem=outer_recv,
                device_id=(owner // batch_count, lax.rem(owner, batch_count)),
                device_id_type=MESH,
            )
            own = pltpu.make_async_copy(summed.at[phase, step], outer_in.at[slot], outer_recv)
            yield (
                jnp.logical_and(valid, owner != me),
                remote,
                jnp.logical_and(valid, owner == me),
                own,
            )

    def turned_copies(late):
        def pick(values):
            return jnp.where(late, values[2], values[0])

        for index in range(len(plan.turned[0])):
            step, there, level = (
                jnp.where(late, *pair)
                for pair in zip(plan.turned[2][index], plan.turned[0][index], strict=True)
            )
            owner = pick(plan.base) + 2 * step + core
            valid = jnp.logical_and(owner >= pick(plan.first), owner <= pick(plan.last))
            gather = pltpu.make_async_remote_copy(
                src_ref=summed.at[2, step],
                dst_ref=turned_in.at[lax.rem(z - level + z_count - 1, z_count)],
                send_sem=turned_send.at[index, 0],
                recv_sem=turned_recv,
                device_id=(space, level * 2 + core),
                device_id_type=MESH,
            )
            deliver = pltpu.make_async_remote_copy(
                src_ref=turned_sum,
                dst_ref=turned_out.at[line - jnp.where(late, 0, 1)],
                send_sem=turned_send.at[index, 1],
                recv_sem=turned_last,
                device_id=(there, batch),
                device_id_type=MESH,
            )
            yield (
                jnp.logical_and(valid, z != level),
                gather,
                jnp.logical_and(valid, z == level),
                deliver,
                step,
            )

    def send_turned(copies):
        for _, _, here, deliver, step in copies:

            @pl.when(here)
            def _():
                pltpu.make_async_copy(turned_in, turned_in, turned_recv).wait()
                turned_sum[...] = summed[2, step] + jnp.sum(turned_in[...], axis=0)
                deliver.start()

    def column_copies():
        for index, (there, steps) in enumerate(plan.middle.items()):
            for step, level in steps:
                yield z != level, pltpu.make_async_remote_copy(
                    src_ref=summed.at[0, step],
                    dst_ref=column_in.at[index, lax.rem(z - level + z_count, z_count) - 1],
                    send_sem=owner_send.at[0, step],
                    recv_sem=column_recv.at[index],
                    device_id=(space, level * 2 + core),
                    device_id_type=MESH,
                )

    def plane_copies():
        for index, (there, steps) in enumerate(plan.middle.items()):
            source, target = column_sum.at[index], middle_in.at[space]
            remote = pltpu.make_async_remote_copy(
                src_ref=source,
                dst_ref=target,
                send_sem=plane_send.at[index],
                recv_sem=middle_recv,
                device_id=(there, batch),
                device_id_type=MESH,
            )
            own = pltpu.make_async_copy(source, target, middle_recv)
            level, top = steps[0][1], steps[-1][1]
            here = jnp.logical_and(z >= level, z <= top)
            yield index, steps[0][0] + z - level, here, there, remote, own

    def send_middle():
        for index, step, here, there, remote, own in plane_copies():

            @pl.when(here)
            def _():
                got = column_in.at[index]
                pltpu.make_async_copy(got, got, column_recv.at[index]).wait()
                column_sum[index] = summed[0, step] + jnp.sum(got[...], axis=0)
                pl.when(space != there)(remote.start)
                pl.when(space == there)(own.start)

    def core_sum(phase):
        core_copy(phase).wait_recv()
        summed[phase] = held[phase, core] + arrived[phase]

    def start_owner(copies):
        for away, remote, here, own in copies:
            pl.when(away)(remote.start)
            pl.when(here)(own.start)

    def spread(phase, copies):
        core_sum(phase)
        start_owner(copies)

    def drain(copies):
        for away, remote, _, _ in copies:
            pl.when(away)(remote.wait_send)

    near_place, far_place = 2 * near, 2 * side
    partial[...] = jnp.zeros(partial.shape, jnp.float32)

    local[0].wait()
    local[1].wait()
    grad_plane(grad_ref[...], 1)
    hidden_plane(pre_ref[...], 1)
    weight_terms(1, 0, plan.write[1])
    pack(0, plan.read[1])
    core_copy(0).start()
    local[2].wait()
    input_terms(1, True)
    core_sum(0)
    pl.semaphore_wait(ready, len(group))
    for away, copy in column_copies():
        pl.when(away)(copy.start)
    for move in grad_moves:
        move[0].start()

    for move in pre_moves:
        pass_on(move)
    hidden_plane(pre_halo[near], near_place)
    near_late = side == 0
    weight_terms(near_place, 1, jnp.where(near_late, plan.write[2], plan.write[0]))
    pack(1, 0)
    core_copy(1).start()
    close = list(owner_copies(1, near_late))
    spread(1, close)

    @pl.when(passes)
    def _():
        for move in grad_moves:
            move[0].wait_recv()
            move[1].start()

    distant = list(owner_copies(2, jnp.logical_not(near_late)))
    turned = list(turned_copies(jnp.logical_not(near_late)))

    @pl.when(gets)
    def _():
        for move in pre_moves:
            move[1].wait_recv()
        hidden_plane(pre_halo[side], far_place)
        weight_terms(far_place, 2, jnp.where(near_late, plan.write[0], plan.write[2]))
        pack(2, 0)
        core_copy(2).start()

    send_middle()

    @pl.when(gets)
    def _():
        core_sum(2)
        for away, gather, _, _, _ in turned:
            pl.when(away)(gather.start)
        start_owner(distant)

    @pl.when(jnp.logical_not(passes))
    def _():
        for move in grad_moves:
            move[0].wait_recv()

    grad_plane(grad_halo[near], near_place)
    input_terms(near_place, False)

    @pl.when(gets)
    def _():
        send_turned(turned)
        for move in grad_moves:
            move[1].wait_recv()
        grad_plane(grad_halo[side], far_place)
        input_terms(far_place, False)

    for row in range(rows):
        plane[pl.ds(row, channels, stride=rows), :] = total[:, row * lanes : (row + 1) * lanes]
    back = plane[0 : channels * rows, :].reshape(channels, rows, lanes)
    act = pre_ref[...].astype(jnp.float32)
    grad_in_ref[...] = (back * jnp.where(act > 0, 1.0, slope)).astype(grad_in_ref.dtype)

    weight_grad_ref[...] = jnp.zeros(weight_grad_ref.shape, jnp.float32)

    def collect(condition, slots, recv):
        @pl.when(condition)
        def _():
            pltpu.make_async_copy(slots, slots, recv).wait()
            weight_grad_ref[...] += jnp.sum(slots[...], axis=0)

    collect(jnp.logical_and(me >= plan.first[1], me <= plan.last[1]), middle_in, middle_recv)
    outer = jnp.logical_or(me <= plan.last[0], me >= plan.first[2])
    inside = jnp.logical_and(me >= batch_count, me < (space_count - 1) * batch_count)
    close_in = outer_in.at[0 : half_count * z_count]
    collect(jnp.logical_and(outer, jnp.logical_not(inside)), outer_in, outer_recv)
    collect(jnp.logical_and(outer, inside), close_in, outer_recv)
    collect(jnp.logical_and(outer, inside), turned_out, turned_last)

    for move in pre_moves + grad_moves:
        move[0].wait_send()
    core_copy(0).wait_send()
    core_copy(1).wait_send()
    for away, copy in column_copies():
        pl.when(away)(copy.wait_send)
    for _, _, here, there, remote, _ in plane_copies():
        pl.when(jnp.logical_and(here, space != there))(remote.wait_send)
    drain(close)

    @pl.when(passes)
    def _():
        for move in pre_moves + grad_moves:
            move[1].wait_send()

    @pl.when(gets)
    def _():
        core_copy(2).wait_send()
        drain(distant)
        for away, gather, here, deliver, _ in turned:
            pl.when(away)(gather.wait_send)
            pl.when(here)(deliver.wait_send)


def fused_device(pre_act, grad_out, weight):
    samples, channels, local_x, rows, lanes = pre_act.shape
    out_chan, taps = grad_out.shape[1], weight.shape[0]
    space_count, batch_count = lax.axis_size("space"), lax.axis_size("batch")
    fits = (
        samples == 1
        and local_x == 1
        and taps == 27
        and rows == 8
        and lanes == 128
        and out_chan == 128
        and channels % 64 == 0
        and space_count % 2 == 0
    )
    if not fits:
        return on_device(pre_act, grad_out, weight)
    count = samples * batch_count * local_x * space_count * rows * lanes
    factor = 1.0 / count**0.5
    total_rows = taps * channels
    plan = plan_for(space_count, batch_count, taps, channels)
    cells = rows * lanes
    widest = max(channels, out_chan)
    bf16, f32 = jnp.bfloat16, jnp.float32
    scratch = [
        pltpu.VMEM((channels, rows, lanes), bf16),
        pltpu.VMEM((out_chan, rows, lanes), bf16),
        pltpu.VMEM((taps, channels, out_chan), bf16),
        pltpu.VMEM((2, channels, rows, lanes), bf16),
        pltpu.VMEM((2, out_chan, rows, lanes), bf16),
        pltpu.VMEM((widest * rows, lanes), f32),
        pltpu.VMEM((3, 3 * channels, cells + 2 * lanes), bf16),
        pltpu.VMEM((3, 3 * out_chan, cells + 2 * lanes), bf16),
        pltpu.VMEM((channels, cells), f32),
    ]
    if plan:
        body = functools.partial(scatter_kernel, (space_count, batch_count), factor, plan)
        owned = plan.block
        block = (plan.block, out_chan)
        pre_cuts, grad_cuts = 4, 4
        scratch += [
            pltpu.VMEM((3, plan.rows, out_chan), f32),
            pltpu.VMEM((3, 2, plan.count, *block), f32),
            pltpu.VMEM((3, plan.count, *block), f32),
            pltpu.VMEM((3, plan.count, *block), f32),
            pltpu.VMEM((len(plan.middle), batch_count // 2 - 1, *block), f32),
            pltpu.VMEM((len(plan.middle), *block), f32),
            pltpu.VMEM((space_count, *block), f32),
            pltpu.VMEM(((space_count - 1) * batch_count // 2, *block), f32),
            pltpu.VMEM((batch_count // 2 - 1, *block), f32),
            pltpu.VMEM(block, f32),
            pltpu.VMEM((space_count // 2 - 1, *block), f32),
            pltpu.SemaphoreType.DMA((3,)),
            *[pltpu.SemaphoreType.DMA((pre_cuts,))] * 4,
            *[pltpu.SemaphoreType.DMA((grad_cuts,))] * 4,
            pltpu.SemaphoreType.DMA((3,)),
            pltpu.SemaphoreType.DMA((3,)),
            pltpu.SemaphoreType.DMA((3, plan.count)),
            pltpu.SemaphoreType.DMA((len(plan.middle),)),
            pltpu.SemaphoreType.DMA((len(plan.middle),)),
            pltpu.SemaphoreType.DMA,
            pltpu.SemaphoreType.DMA,
            pltpu.SemaphoreType.DMA((len(plan.turned[0]), 2)),
            pltpu.SemaphoreType.DMA,
            pltpu.SemaphoreType.DMA,
            pltpu.SemaphoreType.REGULAR,
        ]
    else:
        body = functools.partial(halo_kernel, (space_count, batch_count), factor)
        owned = total_rows
        scratch += [
            pltpu.VMEM((total_rows, out_chan), f32),
            *[pltpu.SemaphoreType.DMA((4,))] * 5,
        ]
    vmem = pl.BlockSpec(memory_space=pltpu.VMEM)
    grad_in, weight_grad = pl.pallas_call(
        body,
        out_shape=(
            jax.ShapeDtypeStruct((channels, rows, lanes), bf16),
            jax.ShapeDtypeStruct((owned, out_chan), f32),
        ),
        in_specs=[pl.BlockSpec(memory_space=pltpu.HBM)] * 3,
        out_specs=(vmem, vmem),
        scratch_shapes=scratch,
        compiler_params=pltpu.CompilerParams(
            collective_id=0, has_side_effects=True, vmem_limit_bytes=48 * 2**20
        ),
    )(
        pltpu.with_memory_space_constraint(pre_act.reshape(channels, rows, lanes), pltpu.HBM),
        pltpu.with_memory_space_constraint(grad_out.reshape(out_chan, rows, lanes), pltpu.HBM),
        pltpu.with_memory_space_constraint(weight, pltpu.HBM),
    )
    grad_in = grad_in.reshape(pre_act.shape)
    if plan:
        return grad_in, weight_grad[: plan.piece].reshape(-1)
    space_part = lax.psum_scatter(
        weight_grad.reshape(-1), "space", scatter_dimension=0, tiled=True
    )
    return grad_in, lax.psum_scatter(space_part, "batch", scatter_dimension=0, tiled=True)


def solution(mesh):
    return jax.shard_map(
        fused_device,
        mesh=mesh,
        in_specs=(
            P("batch", None, "space", None, None),
            P("batch", None, "space", None, None),
            P(),
        ),
        out_specs=(P("batch", None, "space", None, None), P(("space", "batch"))),
        check_vma=False,
    )
```

```python
import functools

import jax
import jax.numpy as jnp
from jax import lax
from jax.experimental import pallas as pl
from jax.experimental.pallas import tpu as pltpu
from jax.sharding import PartitionSpec as P

slope = 0.3


def padded(block, sides, width):
    for axis, dim in sides:
        count = lax.axis_size(axis)
        forward = [(i, i + 1) for i in range(count - 1)]
        backward = [(target, source) for source, target in forward]
        low = lax.ppermute(
            lax.slice_in_dim(block, block.shape[dim] - width, None, axis=dim), axis, forward
        )
        high = lax.ppermute(lax.slice_in_dim(block, 0, width, axis=dim), axis, backward)
        block = jnp.concatenate([low, block, high], axis=dim)
    return block


def leaky(values):
    return jnp.where(values > 0, values, slope * values)


def on_device(pre_act, grad_out, weight):
    local_x = pre_act.shape[2]
    local_y = pre_act.shape[3]
    local_z = pre_act.shape[4]
    count = (
        pre_act.shape[0]
        * lax.axis_size("batch")
        * local_x
        * lax.axis_size("space")
        * local_y
        * local_z
    )
    factor = 1.0 / jnp.sqrt(jnp.float32(count))
    act_float = pre_act.astype(jnp.float32)
    yz_pad = ((0, 0), (0, 0), (0, 0), (1, 1), (1, 1))
    grad_hidden = jnp.zeros(pre_act.shape, jnp.float32)
    tap_grads = []
    joined = jnp.concatenate([pre_act, grad_out], axis=1)
    widened = padded(joined, (("space", 2),), 1)
    in_chan = pre_act.shape[1]
    hidden_pad = jnp.pad(
        leaky(widened[:, :in_chan].astype(jnp.float32)).astype(jnp.bfloat16), yz_pad
    )
    grad_pad = jnp.pad(widened[:, in_chan:], yz_pad)
    for tap in range(27):
        shift_x = tap // 9 - 1
        shift_y = tap // 3 % 3 - 1
        shift_z = tap % 3 - 1
        window = grad_pad[
            :,
            :,
            1 - shift_x : 1 - shift_x + local_x,
            1 - shift_y : 1 - shift_y + local_y,
            1 - shift_z : 1 - shift_z + local_z,
        ]
        grad_hidden = grad_hidden + jnp.einsum(
            "ic,scxyz->sixyz", weight[tap], window, preferred_element_type=jnp.float32
        )
        moved = hidden_pad[
            :,
            :,
            1 + shift_x : 1 + shift_x + local_x,
            1 + shift_y : 1 + shift_y + local_y,
            1 + shift_z : 1 + shift_z + local_z,
        ]
        tap_grads.append(
            jnp.einsum("sixyz,scxyz->ic", moved, grad_out, preferred_element_type=jnp.float32)
        )
    grad_in = (grad_hidden * jnp.where(act_float > 0, 1.0, slope)).astype(jnp.bfloat16)
    partial_sum = (jnp.stack(tap_grads) * factor).reshape(-1)
    space_part = lax.psum_scatter(partial_sum, "space", scatter_dimension=0, tiled=True)
    weight_grad = lax.psum_scatter(space_part, "batch", scatter_dimension=0, tiled=True)
    return (grad_in, weight_grad)


MESH = pl.DeviceIdType.MESH


def prepare(values, scratch, target):
    channels, rows, lanes = values.shape
    scratch[0 : channels * rows, :] = values.reshape(channels * rows, lanes)
    lane = lax.broadcasted_iota(jnp.int32, (channels, lanes), 1)
    blank = jnp.zeros((3 * channels, lanes), target.dtype)
    target[:, 0:lanes] = blank
    target[:, (rows + 1) * lanes : (rows + 2) * lanes] = blank
    for row in range(rows):
        block = scratch[pl.ds(row, channels, stride=rows), :]
        before = jnp.where(lane == 0, 0.0, pltpu.roll(block, 1, 1))
        after = jnp.where(lane == lanes - 1, 0.0, pltpu.roll(block, lanes - 1, 1))
        for place, shifted in enumerate((before, block, after)):
            target[
                place * channels : (place + 1) * channels, (row + 1) * lanes : (row + 2) * lanes
            ] = shifted.astype(target.dtype)


def halo_kernel(
    sizes,
    factor,
    pre_hbm,
    grad_hbm,
    weight_hbm,
    grad_in_ref,
    weight_grad_ref,
    pre_ref,
    grad_ref,
    weight_ref,
    pre_halo,
    grad_halo,
    plane,
    hidden_rows,
    grad_rows,
    total,
    partial,
    local_sem,
    direct_send,
    direct_recv,
    passed_send,
    passed_recv,
):
    space_count, batch_count = sizes
    space, batch = lax.axis_index("space"), lax.axis_index("batch")
    channels, rows, lanes = pre_ref.shape
    out_chan = grad_ref.shape[0]
    cells = rows * lanes

    coords = dict(c=lax.rem(batch, 2), z=batch // 2, x=lax.rem(space, 2), y=space // 2)
    side = coords["x"]

    def peer(axis, place):
        moved = dict(coords, **{axis: place})
        return (moved["y"] * 2 + moved["x"], moved["z"] * 2 + moved["c"])

    local = [
        pltpu.make_async_copy(source, target, local_sem.at[place])
        for place, (source, target) in enumerate(
            ((grad_hbm, grad_ref), (pre_hbm, pre_ref), (weight_hbm, weight_ref))
        )
    ]
    for copy in local:
        copy.start()

    barrier = pltpu.get_barrier_semaphore()
    low, high = space >= 2, space < space_count - 2
    pl.semaphore_signal(
        barrier, inc=1, device_id=peer("x", 1 - side), device_id_type=MESH
    )
    for there, condition in ((space - 2, low), (space + 2, high)):

        @pl.when(condition)
        def _():
            pl.semaphore_signal(barrier, inc=1, device_id=(there, batch), device_id_type=MESH)

    pl.semaphore_wait(barrier, 1 + jnp.where(low, 1, 0) + jnp.where(high, 1, 0))

    half, quarter = out_chan // 2, channels // 2
    messages = [
        (pre_hbm.at[0:quarter], lambda slot: pre_halo.at[slot, 0:quarter]),
        (pre_hbm.at[quarter:channels], lambda slot: pre_halo.at[slot, quarter:channels]),
        (grad_hbm.at[0:half], lambda slot: grad_halo.at[slot, 0:half]),
        (grad_hbm.at[half:out_chan], lambda slot: grad_halo.at[slot, half:out_chan]),
    ]
    near = 1 - side
    passes = jnp.where(side == 0, space < space_count - 2, space >= 2)
    gets = jnp.where(side == 0, space >= 2, space < space_count - 2)
    beyond = jnp.where(side == 0, space + 2, space - 2)

    def direct(index):
        source, slots = messages[index]
        return pltpu.make_async_remote_copy(
            src_ref=source,
            dst_ref=slots(side),
            send_sem=direct_send.at[index],
            recv_sem=direct_recv.at[index],
            device_id=peer("x", 1 - side),
            device_id_type=MESH,
        )

    def passed(index):
        slots = messages[index][1]
        return pltpu.make_async_remote_copy(
            src_ref=slots(near),
            dst_ref=slots(side),
            send_sem=passed_send.at[index],
            recv_sem=passed_recv.at[index],
            device_id=(beyond, batch),
            device_id_type=MESH,
        )

    sent = [direct(index) for index in range(4)]
    for copy in sent:
        copy.start()

    def pass_on(index):
        sent[index].wait_recv()

        @pl.when(passes)
        def _():
            passed(index).start()

    def take(first, target):
        @pl.when(gets)
        def _():
            passed(first).wait_recv()
            passed(first + 1).wait_recv()

        @pl.when(jnp.logical_not(gets))
        def _():
            target[side] = jnp.zeros(target.shape[1:], target.dtype)

    def hidden_plane(values, place):
        prepare(leaky(values.astype(jnp.float32)), plane, hidden_rows.at[place])

    def grad_plane(values, place):
        prepare(values.astype(jnp.float32), plane, grad_rows.at[place])

    def weight_terms(place):
        own = grad_rows[1, out_chan : 2 * out_chan, lanes : lanes + cells]
        for shift_y in (-1, 0, 1):
            start = (9 * place + 3 * (shift_y + 1)) * channels
            if not isinstance(place, int):
                start = pl.multiple_of(start, 8)
            term = lax.dot_general(
                hidden_rows[place, :, (1 + shift_y) * lanes : (1 + shift_y) * lanes + cells],
                own,
                (((1,), (1,)), ((), ())),
                preferred_element_type=jnp.float32,
            )
            partial[pl.ds(start, 3 * channels), :] = term * factor

    def input_terms(place, first):
        for shift_y in (-1, 0, 1):
            tap = 9 * (2 - place) + 3 * (shift_y + 1)
            term = jnp.dot(
                jnp.concatenate([weight_ref[tap + 2], weight_ref[tap + 1], weight_ref[tap]], axis=1),
                grad_rows[place, :, (1 - shift_y) * lanes : (1 - shift_y) * lanes + cells],
                preferred_element_type=jnp.float32,
            )
            if first and shift_y == -1:
                total[...] = term
            else:
                total[...] += term

    near_place, far_place = 2 * near, 2 * side

    local[0].wait()
    local[1].wait()
    grad_plane(grad_ref[...], 1)
    hidden_plane(pre_ref[...], 1)
    pass_on(0)
    pass_on(1)
    weight_terms(1)
    hidden_plane(pre_halo[near], near_place)
    weight_terms(near_place)
    local[2].wait()
    take(0, pre_halo)
    hidden_plane(pre_halo[side], far_place)
    weight_terms(far_place)

    def near_input():
        grad_plane(grad_halo[near], near_place)
        input_terms(near_place, False)

    def far_input():
        take(2, grad_halo)
        grad_plane(grad_halo[side], far_place)
        input_terms(far_place, False)
        for row in range(rows):
            plane[pl.ds(row, channels, stride=rows), :] = total[:, row * lanes : (row + 1) * lanes]
        back = plane[0 : channels * rows, :].reshape(channels, rows, lanes)
        act = pre_ref[...].astype(jnp.float32)
        grad_in_ref[...] = (back * jnp.where(act > 0, 1.0, slope)).astype(grad_in_ref.dtype)

    pass_on(2)
    pass_on(3)
    input_terms(1, True)
    near_input()
    far_input()
    weight_grad_ref[...] = partial[...]

    for copy in sent:
        copy.wait_send()

    @pl.when(passes)
    def _():
        for index in range(4):
            passed(index).wait_send()


class Plan:
    def __init__(self, space_count, batch_count, taps, channels):
        devices = space_count * batch_count
        self.section = taps * channels // 3
        self.piece = 3 * self.section // devices
        self.block = -(-self.piece // 8) * 8
        self.first, self.last, self.base, self.write, self.read = [], [], [], [], []
        for part in range(3):
            start = part * self.section
            first = start // self.piece
            self.first.append(first)
            self.last.append((start + self.section - 1) // self.piece)
            self.base.append(first - first % 2)
            ahead = start - self.piece * self.base[part]
            self.write.append(-(-ahead // 8) * 8)
            self.read.append(self.write[part] - ahead)
        self.count = max(
            (last - base) // 2 + 1 for last, base in zip(self.last, self.base, strict=True)
        )
        reach = self.piece * (2 * self.count - 1) + self.block
        self.turned = [
            [
                (step, owner // batch_count, owner % batch_count // 2)
                for step in range(self.count)
                for owner in [self.base[part] + 2 * step]
                if 0 < owner // batch_count < space_count - 1
                and owner + 1 >= self.first[part]
                and owner <= self.last[part]
            ]
            for part in range(3)
        ]
        self.middle = {}
        for step in range(self.count):
            space, batch = divmod(self.base[1] + 2 * step, batch_count)
            self.middle.setdefault(space, []).append((step, batch // 2))
        self.rows = max(
            max(-(-(read + reach) // 8) * 8, write + self.section)
            for read, write in zip(self.read, self.write, strict=True)
        )


def plan_for(space_count, batch_count, taps, channels):
    devices = space_count * batch_count
    if space_count % 2 or batch_count % 2 or batch_count < 4 or space_count < 4:
        return None
    if taps % 3 or taps * channels % devices or taps * channels // devices < 8:
        return None
    plan = Plan(space_count, batch_count, taps, channels)
    if plan.read[0] or plan.read[2] or plan.last[0] >= plan.first[2]:
        return None
    if len(plan.turned[0]) != len(plan.turned[2]) or not plan.turned[0]:
        return None
    for turned in (plan.turned[0], plan.turned[2]):
        if len({level for _, _, level in turned}) != len(turned):
            return None
    if plan.first[1] != plan.base[1] or plan.last[1] != plan.base[1] + 2 * plan.count - 1:
        return None
    return plan


def scatter_kernel(
    sizes,
    factor,
    plan,
    pre_hbm,
    grad_hbm,
    weight_hbm,
    grad_in_ref,
    weight_grad_ref,
    pre_ref,
    grad_ref,
    weight_ref,
    pre_halo,
    grad_halo,
    plane,
    hidden_rows,
    grad_rows,
    total,
    partial,
    held,
    arrived,
    summed,
    column_in,
    column_sum,
    middle_in,
    outer_in,
    turned_in,
    turned_sum,
    turned_out,
    owned,
    local_sem,
    pre_send,
    pre_recv,
    pre_pass_send,
    pre_pass_recv,
    grad_send,
    grad_recv,
    grad_pass_send,
    grad_pass_recv,
    core_send,
    core_recv,
    owner_send,
    plane_send,
    column_recv,
    middle_recv,
    outer_recv,
    turned_send,
    turned_recv,
    turned_last,
    ready,
):
    space_count, batch_count = sizes
    space, batch = lax.axis_index("space"), lax.axis_index("batch")
    channels, rows, lanes = pre_ref.shape
    out_chan = grad_ref.shape[0]
    cells = rows * lanes
    half_count, z_count = space_count // 2, batch_count // 2
    core, z = lax.rem(batch, 2), batch // 2
    side, line = lax.rem(space, 2), space // 2
    me = space * batch_count + batch
    near = 1 - side
    passes = jnp.where(side == 0, space < space_count - 2, space >= 2)
    gets = jnp.where(side == 0, space >= 2, space < space_count - 2)
    beyond = jnp.where(side == 0, space + 2, space - 2)
    across = (line * 2 + near, batch)
    twin = (space, z * 2 + 1 - core)

    group = [
        (lax.rem(line + step, half_count) * 2 + (side if straight else near), batch)
        for step in range(half_count)
        for straight in (True, False)
        if step or not straight
    ]
    barrier = pltpu.get_barrier_semaphore()
    column = [
        (space, lax.rem(z + step, z_count) * 2 + core) for step in range(1, z_count)
    ]
    for device in [twin, *group, *column]:
        pl.semaphore_signal(barrier, inc=1, device_id=device, device_id_type=MESH)

    local = [
        pltpu.make_async_copy(source, target, local_sem.at[place])
        for place, (source, target) in enumerate(
            ((grad_hbm, grad_ref), (pre_hbm, pre_ref), (weight_hbm, weight_ref))
        )
    ]
    for copy in local:
        copy.start()
    pl.semaphore_wait(barrier, 1 + len(group) + len(column))

    def crossing(source, halo, sems, passed_sems, width, index):
        cut = slice(index * width, (index + 1) * width)
        there = pltpu.make_async_remote_copy(
            src_ref=source.at[cut],
            dst_ref=halo.at[side, cut],
            send_sem=sems[0].at[index],
            recv_sem=sems[1].at[index],
            device_id=across,
            device_id_type=MESH,
        )
        onward = pltpu.make_async_remote_copy(
            src_ref=halo.at[near, cut],
            dst_ref=halo.at[side, cut],
            send_sem=passed_sems[0].at[index],
            recv_sem=passed_sems[1].at[index],
            device_id=(beyond, batch),
            device_id_type=MESH,
        )
        return there, onward

    pre_cuts, grad_cuts = pre_send.shape[0], grad_send.shape[0]
    pre_moves = [
        crossing(
            pre_hbm,
            pre_halo,
            (pre_send, pre_recv),
            (pre_pass_send, pre_pass_recv),
            channels // pre_cuts,
            index,
        )
        for index in range(pre_cuts)
    ]
    grad_moves = [
        crossing(
            grad_hbm,
            grad_halo,
            (grad_send, grad_recv),
            (grad_pass_send, grad_pass_recv),
            out_chan // grad_cuts,
            index,
        )
        for index in range(grad_cuts)
    ]

    def pass_on(move):
        move[0].wait_recv()

        @pl.when(passes)
        def _():
            move[1].start()

    for move in pre_moves:
        move[0].start()
    for device in group:
        pl.semaphore_signal(ready, inc=1, device_id=device, device_id_type=MESH)

    def weight_terms(place, phase, shift):
        own = grad_rows[1, out_chan : 2 * out_chan, lanes : lanes + cells]
        for shift_y in (-1, 0, 1):
            start = shift + 3 * (shift_y + 1) * channels
            if not isinstance(start, int):
                start = pl.multiple_of(start, 8)
            term = lax.dot_general(
                hidden_rows[place, :, (1 + shift_y) * lanes : (1 + shift_y) * lanes + cells],
                own,
                (((1,), (1,)), ((), ())),
                preferred_element_type=jnp.float32,
            )
            partial[phase, pl.ds(start, 3 * channels), :] = term * factor

    def input_terms(place, first):
        for shift_y in (-1, 0, 1):
            tap = 9 * (2 - place) + 3 * (shift_y + 1)
            term = jnp.dot(
                jnp.concatenate([weight_ref[tap + 2], weight_ref[tap + 1], weight_ref[tap]], axis=1),
                grad_rows[place, :, (1 - shift_y) * lanes : (1 - shift_y) * lanes + cells],
                preferred_element_type=jnp.float32,
            )
            if first and shift_y == -1:
                total[...] = term
            else:
                total[...] += term

    def hidden_plane(values, place):
        prepare(leaky(values.astype(jnp.float32)), plane, hidden_rows.at[place])

    def grad_plane(values, place):
        prepare(values.astype(jnp.float32), plane, grad_rows.at[place])

    def core_copy(phase):
        return pltpu.make_async_remote_copy(
            src_ref=held.at[phase, 1 - core],
            dst_ref=arrived.at[phase],
            send_sem=core_send.at[phase],
            recv_sem=core_recv.at[phase],
            device_id=twin,
            device_id_type=MESH,
        )

    def pack(phase, read):
        for parity in range(2):
            for step in range(plan.count):
                start = read + plan.piece * (2 * step + parity)
                held[phase, parity, step] = partial[phase, start : start + plan.block, :]

    def owner_copies(phase, late):
        def pick(values):
            return jnp.where(late, values[2], values[0])

        base, first, last = pick(plan.base), pick(plan.first), pick(plan.last)
        far_slot = line - jnp.where(late, 0, 1)
        slot = (line if phase == 1 else half_count + far_slot) * z_count + z
        for step in range(plan.count):
            owner = base + 2 * step + core
            valid = jnp.logical_and(owner >= first, owner <= last)
            if phase == 2:
                valid = jnp.logical_and(
                    valid,
                    jnp.logical_or(
                        owner < batch_count, owner >= (space_count - 1) * batch_count
                    ),
                )
            remote = pltpu.make_async_remote_copy(
                src_ref=summed.at[phase, step],
                dst_ref=outer_in.at[slot],
                send_sem=owner_send.at[phase, step],
                recv_sem=outer_recv,
                device_id=(owner // batch_count, lax.rem(owner, batch_count)),
                device_id_type=MESH,
            )
            own = pltpu.make_async_copy(summed.at[phase, step], outer_in.at[slot], outer_recv)
            yield (
                jnp.logical_and(valid, owner != me),
                remote,
                jnp.logical_and(valid, owner == me),
                own,
            )

    def turned_copies(late):
        def pick(values):
            return jnp.where(late, values[2], values[0])

        for index in range(len(plan.turned[0])):
            step, there, level = (
                jnp.where(late, *pair)
                for pair in zip(plan.turned[2][index], plan.turned[0][index], strict=True)
            )
            owner = pick(plan.base) + 2 * step + core
            valid = jnp.logical_and(owner >= pick(plan.first), owner <= pick(plan.last))
            gather = pltpu.make_async_remote_copy(
                src_ref=summed.at[2, step],
                dst_ref=turned_in.at[lax.rem(z - level + z_count - 1, z_count)],
                send_sem=turned_send.at[index, 0],
                recv_sem=turned_recv,
                device_id=(space, level * 2 + core),
                device_id_type=MESH,
            )
            deliver = pltpu.make_async_remote_copy(
                src_ref=turned_sum,
                dst_ref=turned_out.at[line - jnp.where(late, 0, 1)],
                send_sem=turned_send.at[index, 1],
                recv_sem=turned_last,
                device_id=(there, batch),
                device_id_type=MESH,
            )
            yield (
                jnp.logical_and(valid, z != level),
                gather,
                jnp.logical_and(valid, z == level),
                deliver,
                step,
            )

    def send_turned(copies):
        for _, _, here, deliver, step in copies:

            @pl.when(here)
            def _():
                pltpu.make_async_copy(turned_in, turned_in, turned_recv).wait()
                turned_sum[...] = summed[2, step] + jnp.sum(turned_in[...], axis=0)
                deliver.start()

    def column_copies():
        for index, (there, steps) in enumerate(plan.middle.items()):
            for step, level in steps:
                yield z != level, pltpu.make_async_remote_copy(
                    src_ref=summed.at[0, step],
                    dst_ref=column_in.at[index, lax.rem(z - level + z_count, z_count) - 1],
                    send_sem=owner_send.at[0, step],
                    recv_sem=column_recv.at[index],
                    device_id=(space, level * 2 + core),
                    device_id_type=MESH,
                )

    def plane_copies():
        for index, (there, steps) in enumerate(plan.middle.items()):
            source, target = column_sum.at[index], middle_in.at[space]
            remote = pltpu.make_async_remote_copy(
                src_ref=source,
                dst_ref=target,
                send_sem=plane_send.at[index],
                recv_sem=middle_recv,
                device_id=(there, batch),
                device_id_type=MESH,
            )
            own = pltpu.make_async_copy(source, target, middle_recv)
            level, top = steps[0][1], steps[-1][1]
            here = jnp.logical_and(z >= level, z <= top)
            yield index, steps[0][0] + z - level, here, there, remote, own

    def send_middle():
        for index, step, here, there, remote, own in plane_copies():

            @pl.when(here)
            def _():
                got = column_in.at[index]
                pltpu.make_async_copy(got, got, column_recv.at[index]).wait()
                column_sum[index] = summed[0, step] + jnp.sum(got[...], axis=0)
                pl.when(space != there)(remote.start)
                pl.when(space == there)(own.start)

    def core_sum(phase):
        core_copy(phase).wait_recv()
        summed[phase] = held[phase, core] + arrived[phase]

    def start_owner(copies):
        for away, remote, here, own in copies:
            pl.when(away)(remote.start)
            pl.when(here)(own.start)

    def spread(phase, copies):
        core_sum(phase)
        start_owner(copies)

    def drain(copies):
        for away, remote, _, _ in copies:
            pl.when(away)(remote.wait_send)

    near_place, far_place = 2 * near, 2 * side
    partial[...] = jnp.zeros(partial.shape, jnp.float32)

    local[0].wait()
    local[1].wait()
    grad_plane(grad_ref[...], 1)
    hidden_plane(pre_ref[...], 1)
    weight_terms(1, 0, plan.write[1])
    pack(0, plan.read[1])
    core_copy(0).start()
    local[2].wait()
    input_terms(1, True)
    core_sum(0)
    pl.semaphore_wait(ready, len(group))
    for away, copy in column_copies():
        pl.when(away)(copy.start)
    for move in grad_moves:
        move[0].start()

    for move in pre_moves:
        pass_on(move)
    hidden_plane(pre_halo[near], near_place)
    near_late = side == 0
    weight_terms(near_place, 1, jnp.where(near_late, plan.write[2], plan.write[0]))
    pack(1, 0)
    core_copy(1).start()
    close = list(owner_copies(1, near_late))
    spread(1, close)

    @pl.when(passes)
    def _():
        for move in grad_moves:
            move[0].wait_recv()
            move[1].start()

    distant = list(owner_copies(2, jnp.logical_not(near_late)))
    turned = list(turned_copies(jnp.logical_not(near_late)))

    @pl.when(gets)
    def _():
        for move in pre_moves:
            move[1].wait_recv()
        hidden_plane(pre_halo[side], far_place)
        weight_terms(far_place, 2, jnp.where(near_late, plan.write[0], plan.write[2]))
        pack(2, 0)
        core_copy(2).start()

    send_middle()

    @pl.when(gets)
    def _():
        core_sum(2)
        for away, gather, _, _, _ in turned:
            pl.when(away)(gather.start)
        start_owner(distant)

    @pl.when(jnp.logical_not(passes))
    def _():
        for move in grad_moves:
            move[0].wait_recv()

    grad_plane(grad_halo[near], near_place)
    input_terms(near_place, False)

    @pl.when(gets)
    def _():
        send_turned(turned)
        for move in grad_moves:
            move[1].wait_recv()
        grad_plane(grad_halo[side], far_place)
        input_terms(far_place, False)

    for row in range(rows):
        plane[pl.ds(row, channels, stride=rows), :] = total[:, row * lanes : (row + 1) * lanes]
    back = plane[0 : channels * rows, :].reshape(channels, rows, lanes)
    act = pre_ref[...].astype(jnp.float32)
    grad_in_ref[...] = (back * jnp.where(act > 0, 1.0, slope)).astype(grad_in_ref.dtype)

    owned[...] = jnp.zeros(owned.shape, jnp.float32)

    def collect(condition, slots, recv):
        @pl.when(condition)
        def _():
            pltpu.make_async_copy(slots, slots, recv).wait()
            owned[...] += jnp.sum(slots[...], axis=0)

    collect(jnp.logical_and(me >= plan.first[1], me <= plan.last[1]), middle_in, middle_recv)
    outer = jnp.logical_or(me <= plan.last[0], me >= plan.first[2])
    inside = jnp.logical_and(me >= batch_count, me < (space_count - 1) * batch_count)
    close_in = outer_in.at[0 : half_count * z_count]
    collect(jnp.logical_and(outer, jnp.logical_not(inside)), outer_in, outer_recv)
    collect(jnp.logical_and(outer, inside), close_in, outer_recv)
    collect(jnp.logical_and(outer, inside), turned_out, turned_last)
    weight_grad_ref[...] = owned[0 : plan.piece, :].reshape(weight_grad_ref.shape)

    for move in pre_moves + grad_moves:
        move[0].wait_send()
    core_copy(0).wait_send()
    core_copy(1).wait_send()
    for away, copy in column_copies():
        pl.when(away)(copy.wait_send)
    for _, _, here, there, remote, _ in plane_copies():
        pl.when(jnp.logical_and(here, space != there))(remote.wait_send)
    drain(close)

    @pl.when(passes)
    def _():
        for move in pre_moves + grad_moves:
            move[1].wait_send()

    @pl.when(gets)
    def _():
        core_copy(2).wait_send()
        drain(distant)
        for away, gather, here, deliver, _ in turned:
            pl.when(away)(gather.wait_send)
            pl.when(here)(deliver.wait_send)


def store_kernel(grad_in_ref, weight_grad_ref, grad_in_hbm, weight_grad_hbm, sems):
    copies = [
        pltpu.make_async_copy(grad_in_ref, grad_in_hbm, sems.at[0]),
        pltpu.make_async_copy(weight_grad_ref, weight_grad_hbm, sems.at[1]),
    ]
    for copy in copies:
        copy.start()
    for copy in copies:
        copy.wait()


def fused_device(pre_act, grad_out, weight):
    samples, channels, local_x, rows, lanes = pre_act.shape
    out_chan, taps = grad_out.shape[1], weight.shape[0]
    space_count, batch_count = lax.axis_size("space"), lax.axis_size("batch")
    fits = (
        samples == 1
        and local_x == 1
        and taps == 27
        and rows == 8
        and lanes == 128
        and out_chan == 128
        and channels % 64 == 0
        and space_count % 2 == 0
    )
    if not fits:
        return on_device(pre_act, grad_out, weight)
    count = samples * batch_count * local_x * space_count * rows * lanes
    factor = 1.0 / count**0.5
    total_rows = taps * channels
    plan = plan_for(space_count, batch_count, taps, channels)
    cells = rows * lanes
    widest = max(channels, out_chan)
    bf16, f32 = jnp.bfloat16, jnp.float32
    scratch = [
        pltpu.VMEM((channels, rows, lanes), bf16),
        pltpu.VMEM((out_chan, rows, lanes), bf16),
        pltpu.VMEM((taps, channels, out_chan), bf16),
        pltpu.VMEM((2, channels, rows, lanes), bf16),
        pltpu.VMEM((2, out_chan, rows, lanes), bf16),
        pltpu.VMEM((widest * rows, lanes), f32),
        pltpu.VMEM((3, 3 * channels, cells + 2 * lanes), bf16),
        pltpu.VMEM((3, 3 * out_chan, cells + 2 * lanes), bf16),
        pltpu.VMEM((channels, cells), f32),
    ]
    if plan:
        body = functools.partial(scatter_kernel, (space_count, batch_count), factor, plan)
        owned = (plan.piece * out_chan,)
        block = (plan.block, out_chan)
        pre_cuts, grad_cuts = 4, 4
        scratch += [
            pltpu.VMEM((3, plan.rows, out_chan), f32),
            pltpu.VMEM((3, 2, plan.count, *block), f32),
            pltpu.VMEM((3, plan.count, *block), f32),
            pltpu.VMEM((3, plan.count, *block), f32),
            pltpu.VMEM((len(plan.middle), batch_count // 2 - 1, *block), f32),
            pltpu.VMEM((len(plan.middle), *block), f32),
            pltpu.VMEM((space_count, *block), f32),
            pltpu.VMEM(((space_count - 1) * batch_count // 2, *block), f32),
            pltpu.VMEM((batch_count // 2 - 1, *block), f32),
            pltpu.VMEM(block, f32),
            pltpu.VMEM((space_count // 2 - 1, *block), f32),
            pltpu.VMEM(block, f32),
            pltpu.SemaphoreType.DMA((3,)),
            *[pltpu.SemaphoreType.DMA((pre_cuts,))] * 4,
            *[pltpu.SemaphoreType.DMA((grad_cuts,))] * 4,
            pltpu.SemaphoreType.DMA((3,)),
            pltpu.SemaphoreType.DMA((3,)),
            pltpu.SemaphoreType.DMA((3, plan.count)),
            pltpu.SemaphoreType.DMA((len(plan.middle),)),
            pltpu.SemaphoreType.DMA((len(plan.middle),)),
            pltpu.SemaphoreType.DMA,
            pltpu.SemaphoreType.DMA,
            pltpu.SemaphoreType.DMA((len(plan.turned[0]), 2)),
            pltpu.SemaphoreType.DMA,
            pltpu.SemaphoreType.DMA,
            pltpu.SemaphoreType.REGULAR,
        ]
    else:
        body = functools.partial(halo_kernel, (space_count, batch_count), factor)
        owned = (total_rows, out_chan)
        scratch += [
            pltpu.VMEM((total_rows, out_chan), f32),
            *[pltpu.SemaphoreType.DMA((4,))] * 5,
        ]
    vmem = pl.BlockSpec(memory_space=pltpu.VMEM)
    grad_in, weight_grad = pl.pallas_call(
        body,
        out_shape=(
            jax.ShapeDtypeStruct((channels, rows, lanes), bf16),
            jax.ShapeDtypeStruct(owned, f32),
        ),
        in_specs=[pl.BlockSpec(memory_space=pltpu.HBM)] * 3,
        out_specs=(vmem, vmem),
        scratch_shapes=scratch,
        compiler_params=pltpu.CompilerParams(
            collective_id=0, has_side_effects=True, vmem_limit_bytes=48 * 2**20
        ),
    )(
        pltpu.with_memory_space_constraint(pre_act.reshape(channels, rows, lanes), pltpu.HBM),
        pltpu.with_memory_space_constraint(grad_out.reshape(out_chan, rows, lanes), pltpu.HBM),
        pltpu.with_memory_space_constraint(weight, pltpu.HBM),
    )
    if plan:
        grad_in, weight_grad = pl.pallas_call(
            store_kernel,
            out_shape=(
                jax.ShapeDtypeStruct(grad_in.shape, bf16),
                jax.ShapeDtypeStruct(weight_grad.shape, f32),
            ),
            in_specs=[vmem] * 2,
            out_specs=[pl.BlockSpec(memory_space=pltpu.HBM)] * 2,
            scratch_shapes=[pltpu.SemaphoreType.DMA((2,))],
        )(
            pltpu.with_memory_space_constraint(grad_in, pltpu.VMEM),
            pltpu.with_memory_space_constraint(weight_grad, pltpu.VMEM),
        )
        return grad_in.reshape(pre_act.shape), weight_grad
    grad_in = grad_in.reshape(pre_act.shape)
    space_part = lax.psum_scatter(
        weight_grad.reshape(-1), "space", scatter_dimension=0, tiled=True
    )
    return grad_in, lax.psum_scatter(space_part, "batch", scatter_dimension=0, tiled=True)


def solution(mesh):
    return jax.shard_map(
        fused_device,
        mesh=mesh,
        in_specs=(
            P("batch", None, "space", None, None),
            P("batch", None, "space", None, None),
            P(),
        ),
        out_specs=(P("batch", None, "space", None, None), P(("space", "batch"))),
        check_vma=False,
    )
```

```python
import functools

import jax
import jax.numpy as jnp
from jax import lax
from jax.experimental import pallas as pl
from jax.experimental.pallas import tpu as pltpu
from jax.sharding import PartitionSpec as P

slope = 0.3


def padded(block, sides, width):
    for axis, dim in sides:
        count = lax.axis_size(axis)
        forward = [(i, i + 1) for i in range(count - 1)]
        backward = [(target, source) for source, target in forward]
        low = lax.ppermute(
            lax.slice_in_dim(block, block.shape[dim] - width, None, axis=dim), axis, forward
        )
        high = lax.ppermute(lax.slice_in_dim(block, 0, width, axis=dim), axis, backward)
        block = jnp.concatenate([low, block, high], axis=dim)
    return block


def leaky(values):
    return jnp.where(values > 0, values, slope * values)


def on_device(pre_act, grad_out, weight):
    local_x = pre_act.shape[2]
    local_y = pre_act.shape[3]
    local_z = pre_act.shape[4]
    count = (
        pre_act.shape[0]
        * lax.axis_size("batch")
        * local_x
        * lax.axis_size("space")
        * local_y
        * local_z
    )
    factor = 1.0 / jnp.sqrt(jnp.float32(count))
    act_float = pre_act.astype(jnp.float32)
    yz_pad = ((0, 0), (0, 0), (0, 0), (1, 1), (1, 1))
    grad_hidden = jnp.zeros(pre_act.shape, jnp.float32)
    tap_grads = []
    joined = jnp.concatenate([pre_act, grad_out], axis=1)
    widened = padded(joined, (("space", 2),), 1)
    in_chan = pre_act.shape[1]
    hidden_pad = jnp.pad(
        leaky(widened[:, :in_chan].astype(jnp.float32)).astype(jnp.bfloat16), yz_pad
    )
    grad_pad = jnp.pad(widened[:, in_chan:], yz_pad)
    for tap in range(27):
        shift_x = tap // 9 - 1
        shift_y = tap // 3 % 3 - 1
        shift_z = tap % 3 - 1
        window = grad_pad[
            :,
            :,
            1 - shift_x : 1 - shift_x + local_x,
            1 - shift_y : 1 - shift_y + local_y,
            1 - shift_z : 1 - shift_z + local_z,
        ]
        grad_hidden = grad_hidden + jnp.einsum(
            "ic,scxyz->sixyz", weight[tap], window, preferred_element_type=jnp.float32
        )
        moved = hidden_pad[
            :,
            :,
            1 + shift_x : 1 + shift_x + local_x,
            1 + shift_y : 1 + shift_y + local_y,
            1 + shift_z : 1 + shift_z + local_z,
        ]
        tap_grads.append(
            jnp.einsum("sixyz,scxyz->ic", moved, grad_out, preferred_element_type=jnp.float32)
        )
    grad_in = (grad_hidden * jnp.where(act_float > 0, 1.0, slope)).astype(jnp.bfloat16)
    partial_sum = (jnp.stack(tap_grads) * factor).reshape(-1)
    space_part = lax.psum_scatter(partial_sum, "space", scatter_dimension=0, tiled=True)
    weight_grad = lax.psum_scatter(space_part, "batch", scatter_dimension=0, tiled=True)
    return (grad_in, weight_grad)


MESH = pl.DeviceIdType.MESH


def prepare(values, scratch, target):
    channels, rows, lanes = values.shape
    scratch[0 : channels * rows, :] = values.reshape(channels * rows, lanes)
    lane = lax.broadcasted_iota(jnp.int32, (channels, lanes), 1)
    blank = jnp.zeros((3 * channels, lanes), target.dtype)
    target[:, 0:lanes] = blank
    target[:, (rows + 1) * lanes : (rows + 2) * lanes] = blank
    for row in range(rows):
        block = scratch[pl.ds(row, channels, stride=rows), :]
        before = jnp.where(lane == 0, 0.0, pltpu.roll(block, 1, 1))
        after = jnp.where(lane == lanes - 1, 0.0, pltpu.roll(block, lanes - 1, 1))
        for place, shifted in enumerate((before, block, after)):
            target[
                place * channels : (place + 1) * channels, (row + 1) * lanes : (row + 2) * lanes
            ] = shifted.astype(target.dtype)


def halo_kernel(
    sizes,
    factor,
    pre_hbm,
    grad_hbm,
    weight_hbm,
    grad_in_ref,
    weight_grad_ref,
    pre_ref,
    grad_ref,
    weight_ref,
    pre_halo,
    grad_halo,
    plane,
    hidden_rows,
    grad_rows,
    total,
    partial,
    local_sem,
    direct_send,
    direct_recv,
    passed_send,
    passed_recv,
):
    space_count, batch_count = sizes
    space, batch = lax.axis_index("space"), lax.axis_index("batch")
    channels, rows, lanes = pre_ref.shape
    out_chan = grad_ref.shape[0]
    cells = rows * lanes

    coords = dict(c=lax.rem(batch, 2), z=batch // 2, x=lax.rem(space, 2), y=space // 2)
    side = coords["x"]

    def peer(axis, place):
        moved = dict(coords, **{axis: place})
        return (moved["y"] * 2 + moved["x"], moved["z"] * 2 + moved["c"])

    local = [
        pltpu.make_async_copy(source, target, local_sem.at[place])
        for place, (source, target) in enumerate(
            ((grad_hbm, grad_ref), (pre_hbm, pre_ref), (weight_hbm, weight_ref))
        )
    ]
    for copy in local:
        copy.start()

    barrier = pltpu.get_barrier_semaphore()
    low, high = space >= 2, space < space_count - 2
    pl.semaphore_signal(
        barrier, inc=1, device_id=peer("x", 1 - side), device_id_type=MESH
    )
    for there, condition in ((space - 2, low), (space + 2, high)):

        @pl.when(condition)
        def _():
            pl.semaphore_signal(barrier, inc=1, device_id=(there, batch), device_id_type=MESH)

    pl.semaphore_wait(barrier, 1 + jnp.where(low, 1, 0) + jnp.where(high, 1, 0))

    half, quarter = out_chan // 2, channels // 2
    messages = [
        (pre_hbm.at[0:quarter], lambda slot: pre_halo.at[slot, 0:quarter]),
        (pre_hbm.at[quarter:channels], lambda slot: pre_halo.at[slot, quarter:channels]),
        (grad_hbm.at[0:half], lambda slot: grad_halo.at[slot, 0:half]),
        (grad_hbm.at[half:out_chan], lambda slot: grad_halo.at[slot, half:out_chan]),
    ]
    near = 1 - side
    passes = jnp.where(side == 0, space < space_count - 2, space >= 2)
    gets = jnp.where(side == 0, space >= 2, space < space_count - 2)
    beyond = jnp.where(side == 0, space + 2, space - 2)

    def direct(index):
        source, slots = messages[index]
        return pltpu.make_async_remote_copy(
            src_ref=source,
            dst_ref=slots(side),
            send_sem=direct_send.at[index],
            recv_sem=direct_recv.at[index],
            device_id=peer("x", 1 - side),
            device_id_type=MESH,
        )

    def passed(index):
        slots = messages[index][1]
        return pltpu.make_async_remote_copy(
            src_ref=slots(near),
            dst_ref=slots(side),
            send_sem=passed_send.at[index],
            recv_sem=passed_recv.at[index],
            device_id=(beyond, batch),
            device_id_type=MESH,
        )

    sent = [direct(index) for index in range(4)]
    for copy in sent:
        copy.start()

    def pass_on(index):
        sent[index].wait_recv()

        @pl.when(passes)
        def _():
            passed(index).start()

    def take(first, target):
        @pl.when(gets)
        def _():
            passed(first).wait_recv()
            passed(first + 1).wait_recv()

        @pl.when(jnp.logical_not(gets))
        def _():
            target[side] = jnp.zeros(target.shape[1:], target.dtype)

    def hidden_plane(values, place):
        prepare(leaky(values.astype(jnp.float32)), plane, hidden_rows.at[place])

    def grad_plane(values, place):
        prepare(values.astype(jnp.float32), plane, grad_rows.at[place])

    def weight_terms(place):
        own = grad_rows[1, out_chan : 2 * out_chan, lanes : lanes + cells]
        for shift_y in (-1, 0, 1):
            start = (9 * place + 3 * (shift_y + 1)) * channels
            if not isinstance(place, int):
                start = pl.multiple_of(start, 8)
            term = lax.dot_general(
                hidden_rows[place, :, (1 + shift_y) * lanes : (1 + shift_y) * lanes + cells],
                own,
                (((1,), (1,)), ((), ())),
                preferred_element_type=jnp.float32,
            )
            partial[pl.ds(start, 3 * channels), :] = term * factor

    def input_terms(place, first):
        for shift_y in (-1, 0, 1):
            tap = 9 * (2 - place) + 3 * (shift_y + 1)
            term = jnp.dot(
                jnp.concatenate([weight_ref[tap + 2], weight_ref[tap + 1], weight_ref[tap]], axis=1),
                grad_rows[place, :, (1 - shift_y) * lanes : (1 - shift_y) * lanes + cells],
                preferred_element_type=jnp.float32,
            )
            if first and shift_y == -1:
                total[...] = term
            else:
                total[...] += term

    near_place, far_place = 2 * near, 2 * side

    local[0].wait()
    local[1].wait()
    grad_plane(grad_ref[...], 1)
    hidden_plane(pre_ref[...], 1)
    pass_on(0)
    pass_on(1)
    weight_terms(1)
    hidden_plane(pre_halo[near], near_place)
    weight_terms(near_place)
    local[2].wait()
    take(0, pre_halo)
    hidden_plane(pre_halo[side], far_place)
    weight_terms(far_place)

    def near_input():
        grad_plane(grad_halo[near], near_place)
        input_terms(near_place, False)

    def far_input():
        take(2, grad_halo)
        grad_plane(grad_halo[side], far_place)
        input_terms(far_place, False)
        for row in range(rows):
            plane[pl.ds(row, channels, stride=rows), :] = total[:, row * lanes : (row + 1) * lanes]
        back = plane[0 : channels * rows, :].reshape(channels, rows, lanes)
        act = pre_ref[...].astype(jnp.float32)
        grad_in_ref[...] = (back * jnp.where(act > 0, 1.0, slope)).astype(grad_in_ref.dtype)

    pass_on(2)
    pass_on(3)
    input_terms(1, True)
    near_input()
    far_input()
    weight_grad_ref[...] = partial[...]

    for copy in sent:
        copy.wait_send()

    @pl.when(passes)
    def _():
        for index in range(4):
            passed(index).wait_send()


class Plan:
    def __init__(self, space_count, batch_count, taps, channels):
        devices = space_count * batch_count
        self.section = taps * channels // 3
        self.piece = 3 * self.section // devices
        self.block = -(-self.piece // 8) * 8
        self.first, self.last, self.base, self.write, self.read = [], [], [], [], []
        for part in range(3):
            start = part * self.section
            first = start // self.piece
            self.first.append(first)
            self.last.append((start + self.section - 1) // self.piece)
            self.base.append(first - first % 2)
            ahead = start - self.piece * self.base[part]
            self.write.append(-(-ahead // 8) * 8)
            self.read.append(self.write[part] - ahead)
        self.count = max(
            (last - base) // 2 + 1 for last, base in zip(self.last, self.base, strict=True)
        )
        reach = self.piece * (2 * self.count - 1) + self.block
        self.turned = [
            [
                (step, owner // batch_count, owner % batch_count // 2)
                for step in range(self.count)
                for owner in [self.base[part] + 2 * step]
                if 0 < owner // batch_count < space_count - 1
                and owner + 1 >= self.first[part]
                and owner <= self.last[part]
            ]
            for part in range(3)
        ]
        self.middle = {}
        for step in range(self.count):
            space, batch = divmod(self.base[1] + 2 * step, batch_count)
            self.middle.setdefault(space, []).append((step, batch // 2))
        self.rows = max(
            max(-(-(read + reach) // 8) * 8, write + self.section)
            for read, write in zip(self.read, self.write, strict=True)
        )


def plan_for(space_count, batch_count, taps, channels):
    devices = space_count * batch_count
    if space_count % 2 or batch_count % 2 or batch_count < 4 or space_count < 4:
        return None
    if taps % 3 or taps * channels % devices or taps * channels // devices < 8:
        return None
    plan = Plan(space_count, batch_count, taps, channels)
    if plan.read[0] or plan.read[2] or plan.last[0] >= plan.first[2]:
        return None
    if len(plan.turned[0]) != len(plan.turned[2]) or not plan.turned[0]:
        return None
    for turned in (plan.turned[0], plan.turned[2]):
        if len({level for _, _, level in turned}) != len(turned):
            return None
    if plan.first[1] != plan.base[1] or plan.last[1] != plan.base[1] + 2 * plan.count - 1:
        return None
    return plan


def scatter_kernel(
    sizes,
    factor,
    plan,
    pre_hbm,
    grad_hbm,
    weight_hbm,
    grad_in_ref,
    weight_grad_ref,
    pre_ref,
    grad_ref,
    weight_ref,
    pre_halo,
    grad_halo,
    plane,
    hidden_rows,
    grad_rows,
    total,
    partial,
    held,
    arrived,
    summed,
    column_in,
    column_sum,
    middle_in,
    outer_in,
    turned_in,
    turned_sum,
    turned_out,
    owned,
    local_sem,
    pre_send,
    pre_recv,
    pre_pass_send,
    pre_pass_recv,
    grad_send,
    grad_recv,
    grad_pass_send,
    grad_pass_recv,
    core_send,
    core_recv,
    owner_send,
    plane_send,
    column_recv,
    middle_recv,
    outer_recv,
    turned_send,
    turned_recv,
    turned_last,
    ready,
):
    space_count, batch_count = sizes
    space, batch = lax.axis_index("space"), lax.axis_index("batch")
    channels, rows, lanes = pre_ref.shape
    out_chan = grad_ref.shape[0]
    cells = rows * lanes
    half_count, z_count = space_count // 2, batch_count // 2
    core, z = lax.rem(batch, 2), batch // 2
    side, line = lax.rem(space, 2), space // 2
    me = space * batch_count + batch
    near = 1 - side
    passes = jnp.where(side == 0, space < space_count - 2, space >= 2)
    gets = jnp.where(side == 0, space >= 2, space < space_count - 2)
    beyond = jnp.where(side == 0, space + 2, space - 2)
    across = (line * 2 + near, batch)
    twin = (space, z * 2 + 1 - core)

    group = [
        (lax.rem(line + step, half_count) * 2 + (side if straight else near), batch)
        for step in range(half_count)
        for straight in (True, False)
        if step or not straight
    ]
    barrier = pltpu.get_barrier_semaphore()
    column = [
        (space, lax.rem(z + step, z_count) * 2 + core) for step in range(1, z_count)
    ]
    for device in [twin, *group, *column]:
        pl.semaphore_signal(barrier, inc=1, device_id=device, device_id_type=MESH)

    local = [
        pltpu.make_async_copy(source, target, local_sem.at[place])
        for place, (source, target) in enumerate(
            ((grad_hbm, grad_ref), (pre_hbm, pre_ref), (weight_hbm, weight_ref))
        )
    ]
    for copy in local:
        copy.start()
    pl.semaphore_wait(barrier, 1 + len(group) + len(column))

    def crossing(source, halo, sems, passed_sems, width, index):
        cut = slice(index * width, (index + 1) * width)
        there = pltpu.make_async_remote_copy(
            src_ref=source.at[cut],
            dst_ref=halo.at[side, cut],
            send_sem=sems[0].at[index],
            recv_sem=sems[1].at[index],
            device_id=across,
            device_id_type=MESH,
        )
        onward = pltpu.make_async_remote_copy(
            src_ref=halo.at[near, cut],
            dst_ref=halo.at[side, cut],
            send_sem=passed_sems[0].at[index],
            recv_sem=passed_sems[1].at[index],
            device_id=(beyond, batch),
            device_id_type=MESH,
        )
        return there, onward

    pre_cuts, grad_cuts = pre_send.shape[0], grad_send.shape[0]
    pre_moves = [
        crossing(
            pre_hbm,
            pre_halo,
            (pre_send, pre_recv),
            (pre_pass_send, pre_pass_recv),
            channels // pre_cuts,
            index,
        )
        for index in range(pre_cuts)
    ]
    grad_moves = [
        crossing(
            grad_hbm,
            grad_halo,
            (grad_send, grad_recv),
            (grad_pass_send, grad_pass_recv),
            out_chan // grad_cuts,
            index,
        )
        for index in range(grad_cuts)
    ]

    def pass_on(move):
        move[0].wait_recv()

        @pl.when(passes)
        def _():
            move[1].start()

    for move in pre_moves:
        move[0].start()
    for device in group:
        pl.semaphore_signal(ready, inc=1, device_id=device, device_id_type=MESH)

    def weight_terms(place, phase, shift):
        own = grad_rows[1, out_chan : 2 * out_chan, lanes : lanes + cells]
        for shift_y in (-1, 0, 1):
            start = shift + 3 * (shift_y + 1) * channels
            if not isinstance(start, int):
                start = pl.multiple_of(start, 8)
            term = lax.dot_general(
                hidden_rows[place, :, (1 + shift_y) * lanes : (1 + shift_y) * lanes + cells],
                own,
                (((1,), (1,)), ((), ())),
                preferred_element_type=jnp.float32,
            )
            partial[phase, pl.ds(start, 3 * channels), :] = term * factor

    def input_terms(place, first):
        for shift_y in (-1, 0, 1):
            tap = 9 * (2 - place) + 3 * (shift_y + 1)
            term = jnp.dot(
                jnp.concatenate([weight_ref[tap + 2], weight_ref[tap + 1], weight_ref[tap]], axis=1),
                grad_rows[place, :, (1 - shift_y) * lanes : (1 - shift_y) * lanes + cells],
                preferred_element_type=jnp.float32,
            )
            if first and shift_y == -1:
                total[...] = term
            else:
                total[...] += term

    def hidden_plane(values, place):
        prepare(leaky(values.astype(jnp.float32)), plane, hidden_rows.at[place])

    def grad_plane(values, place):
        prepare(values.astype(jnp.float32), plane, grad_rows.at[place])

    def core_copy(phase):
        return pltpu.make_async_remote_copy(
            src_ref=held.at[phase, 1 - core],
            dst_ref=arrived.at[phase],
            send_sem=core_send.at[phase],
            recv_sem=core_recv.at[phase],
            device_id=twin,
            device_id_type=MESH,
        )

    def pack(phase, read):
        for parity in range(2):
            for step in range(plan.count):
                start = read + plan.piece * (2 * step + parity)
                held[phase, parity, step] = partial[phase, start : start + plan.block, :]

    def owner_copies(phase, late):
        def pick(values):
            return jnp.where(late, values[2], values[0])

        base, first, last = pick(plan.base), pick(plan.first), pick(plan.last)
        far_slot = line - jnp.where(late, 0, 1)
        slot = (line if phase == 1 else half_count + far_slot) * z_count + z
        for step in range(plan.count):
            owner = base + 2 * step + core
            valid = jnp.logical_and(owner >= first, owner <= last)
            outermost = jnp.logical_or(
                owner < batch_count, owner >= (space_count - 1) * batch_count
            )
            valid = jnp.logical_and(valid, outermost)
            remote = pltpu.make_async_remote_copy(
                src_ref=summed.at[phase, step],
                dst_ref=outer_in.at[slot],
                send_sem=owner_send.at[phase, step],
                recv_sem=outer_recv,
                device_id=(owner // batch_count, lax.rem(owner, batch_count)),
                device_id_type=MESH,
            )
            own = pltpu.make_async_copy(summed.at[phase, step], outer_in.at[slot], outer_recv)
            yield (
                jnp.logical_and(valid, owner != me),
                remote,
                jnp.logical_and(valid, owner == me),
                own,
            )

    def turned_copies(phase, late):
        def pick(values):
            return jnp.where(late, values[2], values[0])

        for index in range(len(plan.turned[0])):
            step, there, level = (
                jnp.where(late, *pair)
                for pair in zip(plan.turned[2][index], plan.turned[0][index], strict=True)
            )
            owner = pick(plan.base) + 2 * step + core
            valid = jnp.logical_and(owner >= pick(plan.first), owner <= pick(plan.last))
            gather = pltpu.make_async_remote_copy(
                src_ref=summed.at[phase, step],
                dst_ref=turned_in.at[phase - 1, lax.rem(z - level + z_count - 1, z_count)],
                send_sem=turned_send.at[phase - 1, index, 0],
                recv_sem=turned_recv.at[phase - 1],
                device_id=(space, level * 2 + core),
                device_id_type=MESH,
            )
            place = line if phase == 1 else half_count + line - jnp.where(late, 0, 1)
            deliver = pltpu.make_async_remote_copy(
                src_ref=turned_sum.at[phase - 1],
                dst_ref=turned_out.at[place],
                send_sem=turned_send.at[phase - 1, index, 1],
                recv_sem=turned_last,
                device_id=(there, batch),
                device_id_type=MESH,
            )
            own = pltpu.make_async_copy(
                turned_sum.at[phase - 1], turned_out.at[place], turned_last
            )
            here = jnp.logical_and(valid, z == level)
            yield jnp.logical_and(valid, z != level), gather, here, there, deliver, own, step

    def send_turned(phase, copies):
        for _, _, here, there, deliver, own, step in copies:

            @pl.when(here)
            def _():
                got = turned_in.at[phase - 1]
                pltpu.make_async_copy(got, got, turned_recv.at[phase - 1]).wait()
                turned_sum[phase - 1] = summed[phase, step] + jnp.sum(got[...], axis=0)
                pl.when(space != there)(deliver.start)
                pl.when(space == there)(own.start)

    def drain_turned(copies):
        for away, gather, here, there, deliver, _, _ in copies:
            pl.when(away)(gather.wait_send)
            pl.when(jnp.logical_and(here, space != there))(deliver.wait_send)

    def column_copies():
        for index, (there, steps) in enumerate(plan.middle.items()):
            for step, level in steps:
                yield z != level, pltpu.make_async_remote_copy(
                    src_ref=summed.at[0, step],
                    dst_ref=column_in.at[index, lax.rem(z - level + z_count, z_count) - 1],
                    send_sem=owner_send.at[0, step],
                    recv_sem=column_recv.at[index],
                    device_id=(space, level * 2 + core),
                    device_id_type=MESH,
                )

    def plane_copies():
        for index, (there, steps) in enumerate(plan.middle.items()):
            source, target = column_sum.at[index], middle_in.at[space]
            remote = pltpu.make_async_remote_copy(
                src_ref=source,
                dst_ref=target,
                send_sem=plane_send.at[index],
                recv_sem=middle_recv,
                device_id=(there, batch),
                device_id_type=MESH,
            )
            own = pltpu.make_async_copy(source, target, middle_recv)
            level, top = steps[0][1], steps[-1][1]
            here = jnp.logical_and(z >= level, z <= top)
            yield index, steps[0][0] + z - level, here, there, remote, own

    def send_middle():
        for index, step, here, there, remote, own in plane_copies():

            @pl.when(here)
            def _():
                got = column_in.at[index]
                pltpu.make_async_copy(got, got, column_recv.at[index]).wait()
                column_sum[index] = summed[0, step] + jnp.sum(got[...], axis=0)
                pl.when(space != there)(remote.start)
                pl.when(space == there)(own.start)

    def core_sum(phase):
        core_copy(phase).wait_recv()
        summed[phase] = held[phase, core] + arrived[phase]

    def start_owner(copies):
        for away, remote, here, own in copies:
            pl.when(away)(remote.start)
            pl.when(here)(own.start)

    def drain(copies):
        for away, remote, _, _ in copies:
            pl.when(away)(remote.wait_send)

    near_place, far_place = 2 * near, 2 * side
    partial[...] = jnp.zeros(partial.shape, jnp.float32)

    local[0].wait()
    local[1].wait()
    grad_plane(grad_ref[...], 1)
    hidden_plane(pre_ref[...], 1)
    weight_terms(1, 0, plan.write[1])
    pack(0, plan.read[1])
    core_copy(0).start()
    local[2].wait()
    input_terms(1, True)
    core_sum(0)
    pl.semaphore_wait(ready, len(group))
    for away, copy in column_copies():
        pl.when(away)(copy.start)
    for move in grad_moves:
        move[0].start()

    for move in pre_moves:
        pass_on(move)
    hidden_plane(pre_halo[near], near_place)
    near_late = side == 0
    weight_terms(near_place, 1, jnp.where(near_late, plan.write[2], plan.write[0]))
    pack(1, 0)
    core_copy(1).start()
    close = list(owner_copies(1, near_late))
    core_sum(1)
    turning = list(turned_copies(1, near_late))
    for away, gather, *_ in turning:
        pl.when(away)(gather.start)
    start_owner(close)

    @pl.when(passes)
    def _():
        for move in grad_moves:
            move[0].wait_recv()
            move[1].start()

    distant = list(owner_copies(2, jnp.logical_not(near_late)))
    turned = list(turned_copies(2, jnp.logical_not(near_late)))

    @pl.when(gets)
    def _():
        for move in pre_moves:
            move[1].wait_recv()
        hidden_plane(pre_halo[side], far_place)
        weight_terms(far_place, 2, jnp.where(near_late, plan.write[0], plan.write[2]))
        pack(2, 0)
        core_copy(2).start()

    send_middle()

    @pl.when(gets)
    def _():
        core_sum(2)
        for away, gather, *_ in turned:
            pl.when(away)(gather.start)
        start_owner(distant)

    send_turned(1, turning)

    @pl.when(jnp.logical_not(passes))
    def _():
        for move in grad_moves:
            move[0].wait_recv()

    grad_plane(grad_halo[near], near_place)
    input_terms(near_place, False)

    @pl.when(gets)
    def _():
        send_turned(2, turned)
        for move in grad_moves:
            move[1].wait_recv()
        grad_plane(grad_halo[side], far_place)
        input_terms(far_place, False)

    for row in range(rows):
        plane[pl.ds(row, channels, stride=rows), :] = total[:, row * lanes : (row + 1) * lanes]
    back = plane[0 : channels * rows, :].reshape(channels, rows, lanes)
    act = pre_ref[...].astype(jnp.float32)
    grad_in_ref[...] = (back * jnp.where(act > 0, 1.0, slope)).astype(grad_in_ref.dtype)

    owned[...] = jnp.zeros(owned.shape, jnp.float32)

    def collect(condition, slots, recv):
        @pl.when(condition)
        def _():
            pltpu.make_async_copy(slots, slots, recv).wait()
            owned[...] += jnp.sum(slots[...], axis=0)

    collect(jnp.logical_and(me >= plan.first[1], me <= plan.last[1]), middle_in, middle_recv)
    outer = jnp.logical_or(me <= plan.last[0], me >= plan.first[2])
    inside = jnp.logical_and(me >= batch_count, me < (space_count - 1) * batch_count)
    collect(jnp.logical_and(outer, jnp.logical_not(inside)), outer_in, outer_recv)
    collect(jnp.logical_and(outer, inside), turned_out, turned_last)
    weight_grad_ref[...] = owned[0 : plan.piece, :].reshape(weight_grad_ref.shape)

    for move in pre_moves + grad_moves:
        move[0].wait_send()
    core_copy(0).wait_send()
    core_copy(1).wait_send()
    for away, copy in column_copies():
        pl.when(away)(copy.wait_send)
    for _, _, here, there, remote, _ in plane_copies():
        pl.when(jnp.logical_and(here, space != there))(remote.wait_send)
    drain(close)
    drain_turned(turning)

    @pl.when(passes)
    def _():
        for move in pre_moves + grad_moves:
            move[1].wait_send()

    @pl.when(gets)
    def _():
        core_copy(2).wait_send()
        drain(distant)
        drain_turned(turned)


def store_kernel(grad_in_ref, weight_grad_ref, grad_in_hbm, weight_grad_hbm, sems):
    copies = [
        pltpu.make_async_copy(grad_in_ref, grad_in_hbm, sems.at[0]),
        pltpu.make_async_copy(weight_grad_ref, weight_grad_hbm, sems.at[1]),
    ]
    for copy in copies:
        copy.start()
    for copy in copies:
        copy.wait()


def fused_device(pre_act, grad_out, weight):
    samples, channels, local_x, rows, lanes = pre_act.shape
    out_chan, taps = grad_out.shape[1], weight.shape[0]
    space_count, batch_count = lax.axis_size("space"), lax.axis_size("batch")
    fits = (
        samples == 1
        and local_x == 1
        and taps == 27
        and rows == 8
        and lanes == 128
        and out_chan == 128
        and channels % 64 == 0
        and space_count % 2 == 0
    )
    if not fits:
        return on_device(pre_act, grad_out, weight)
    count = samples * batch_count * local_x * space_count * rows * lanes
    factor = 1.0 / count**0.5
    total_rows = taps * channels
    plan = plan_for(space_count, batch_count, taps, channels)
    cells = rows * lanes
    widest = max(channels, out_chan)
    bf16, f32 = jnp.bfloat16, jnp.float32
    scratch = [
        pltpu.VMEM((channels, rows, lanes), bf16),
        pltpu.VMEM((out_chan, rows, lanes), bf16),
        pltpu.VMEM((taps, channels, out_chan), bf16),
        pltpu.VMEM((2, channels, rows, lanes), bf16),
        pltpu.VMEM((2, out_chan, rows, lanes), bf16),
        pltpu.VMEM((widest * rows, lanes), f32),
        pltpu.VMEM((3, 3 * channels, cells + 2 * lanes), bf16),
        pltpu.VMEM((3, 3 * out_chan, cells + 2 * lanes), bf16),
        pltpu.VMEM((channels, cells), f32),
    ]
    if plan:
        body = functools.partial(scatter_kernel, (space_count, batch_count), factor, plan)
        owned = (plan.piece * out_chan,)
        block = (plan.block, out_chan)
        pre_cuts, grad_cuts = 4, 4
        scratch += [
            pltpu.VMEM((3, plan.rows, out_chan), f32),
            pltpu.VMEM((3, 2, plan.count, *block), f32),
            pltpu.VMEM((3, plan.count, *block), f32),
            pltpu.VMEM((3, plan.count, *block), f32),
            pltpu.VMEM((len(plan.middle), batch_count // 2 - 1, *block), f32),
            pltpu.VMEM((len(plan.middle), *block), f32),
            pltpu.VMEM((space_count, *block), f32),
            pltpu.VMEM(((space_count - 1) * batch_count // 2, *block), f32),
            pltpu.VMEM((2, batch_count // 2 - 1, *block), f32),
            pltpu.VMEM((2, *block), f32),
            pltpu.VMEM((space_count - 1, *block), f32),
            pltpu.VMEM(block, f32),
            pltpu.SemaphoreType.DMA((3,)),
            *[pltpu.SemaphoreType.DMA((pre_cuts,))] * 4,
            *[pltpu.SemaphoreType.DMA((grad_cuts,))] * 4,
            pltpu.SemaphoreType.DMA((3,)),
            pltpu.SemaphoreType.DMA((3,)),
            pltpu.SemaphoreType.DMA((3, plan.count)),
            pltpu.SemaphoreType.DMA((len(plan.middle),)),
            pltpu.SemaphoreType.DMA((len(plan.middle),)),
            pltpu.SemaphoreType.DMA,
            pltpu.SemaphoreType.DMA,
            pltpu.SemaphoreType.DMA((2, len(plan.turned[0]), 2)),
            pltpu.SemaphoreType.DMA((2,)),
            pltpu.SemaphoreType.DMA,
            pltpu.SemaphoreType.REGULAR,
        ]
    else:
        body = functools.partial(halo_kernel, (space_count, batch_count), factor)
        owned = (total_rows, out_chan)
        scratch += [
            pltpu.VMEM((total_rows, out_chan), f32),
            *[pltpu.SemaphoreType.DMA((4,))] * 5,
        ]
    vmem = pl.BlockSpec(memory_space=pltpu.VMEM)
    grad_in, weight_grad = pl.pallas_call(
        body,
        out_shape=(
            jax.ShapeDtypeStruct((channels, rows, lanes), bf16),
            jax.ShapeDtypeStruct(owned, f32),
        ),
        in_specs=[pl.BlockSpec(memory_space=pltpu.HBM)] * 3,
        out_specs=(vmem, vmem),
        scratch_shapes=scratch,
        compiler_params=pltpu.CompilerParams(
            collective_id=0, has_side_effects=True, vmem_limit_bytes=48 * 2**20
        ),
    )(
        pltpu.with_memory_space_constraint(pre_act.reshape(channels, rows, lanes), pltpu.HBM),
        pltpu.with_memory_space_constraint(grad_out.reshape(out_chan, rows, lanes), pltpu.HBM),
        pltpu.with_memory_space_constraint(weight, pltpu.HBM),
    )
    if plan:
        grad_in, weight_grad = pl.pallas_call(
            store_kernel,
            out_shape=(
                jax.ShapeDtypeStruct(grad_in.shape, bf16),
                jax.ShapeDtypeStruct(weight_grad.shape, f32),
            ),
            in_specs=[vmem] * 2,
            out_specs=[pl.BlockSpec(memory_space=pltpu.HBM)] * 2,
            scratch_shapes=[pltpu.SemaphoreType.DMA((2,))],
        )(
            pltpu.with_memory_space_constraint(grad_in, pltpu.VMEM),
            pltpu.with_memory_space_constraint(weight_grad, pltpu.VMEM),
        )
        return grad_in.reshape(pre_act.shape), weight_grad
    grad_in = grad_in.reshape(pre_act.shape)
    space_part = lax.psum_scatter(
        weight_grad.reshape(-1), "space", scatter_dimension=0, tiled=True
    )
    return grad_in, lax.psum_scatter(space_part, "batch", scatter_dimension=0, tiled=True)


def solution(mesh):
    return jax.shard_map(
        fused_device,
        mesh=mesh,
        in_specs=(
            P("batch", None, "space", None, None),
            P("batch", None, "space", None, None),
            P(),
        ),
        out_specs=(P("batch", None, "space", None, None), P(("space", "batch"))),
        check_vma=False,
    )
```
